32 devices in a mesh: dp: 8 (over y, x, core), tensor: 4 (over z).
Axes of the slice: x: 2, y: 2, z: 4, core: 2. Of those that a mesh axis runs over, the one named last changes fastest.
Arguments:
- tokens: bfloat16 [2, 16, 10, 64, 1024], P(None, 'dp', None, 'tensor'), may hold values from -6 to 6
- conditioning: bfloat16 [2, 16, 1024], P(None, 'dp'), may hold values from -6 to 6
- frame_counts: int32 [2, 16], P(None, 'dp'), may hold values from 2 to 9, as said below
- w_qkv: bfloat16 [1024, 3, 1024], P('dp', None, 'tensor'), may hold values from -0.1875 to 0.1875
- w_out: bfloat16 [1024, 1024], P('dp', 'tensor'), may hold values from -1.5 to 1.5
- w_up: bfloat16 [1024, 4096], P('dp', 'tensor'), may hold values from -0.1875 to 0.1875
- w_down: bfloat16 [1024, 4096], P('dp', 'tensor'), may hold values from -0.09375 to 0.09375
- w_ada: bfloat16 [1024, 6144], P('dp', 'tensor'), may hold values from -0.1875 to 0.1875
- pos_table: float32 [16, 2025], P('tensor'), may hold values from -4 to 4
- cotangent: bfloat16 [2, 16, 10, 64, 1024], P(None, 'dp', None, 'tensor'), may hold values from -6 to 6
Outputs:
- block_out: bfloat16 [2, 16, 10, 64, 1024], P(None, 'dp', None, 'tensor')
- grad_tokens: bfloat16 [2, 16, 10, 64, 1024], P(None, 'dp', None, 'tensor')
- grad_cond: float32 [2, 16, 1024], P(None, 'dp')
- grad_w_qkv: float32 [1024, 3, 1024], P('dp', None, 'tensor')
- grad_w_out: float32 [1024, 1024], P('dp', 'tensor')
- grad_w_up: float32 [1024, 4096], P('dp', 'tensor')
- grad_w_down: float32 [1024, 4096], P('dp', 'tensor')
- grad_w_ada: float32 [1024, 6144], P('dp', 'tensor')
- grad_table: float32 [16, 2025], P('tensor')
The draws below stay inside these ranges and needn't reach their ends.
Inputs may be any that keep to these rules, and one draw needn't show every extreme that they name: `frame_counts`: given frames of each clip; in every draw one clip has 2 and another 10 - 1.
All inputs are finite; a program needn't handle non-finite values.
Results may differ from the reference program's by a relative error of at most 0.018.
The reference program's roundings to bfloat16 on the way count: a program that leaves them out, or rounds other values in their place, can miss the bound.
Values may be sent and summed in bfloat16 or wider, within the bound.
No kernel may reach another device: no remote copies, remote signals or barrier semaphores. Data moves between devices by JAX's collectives and lax.ppermute only.
A program may use at most 192 MiB of HBM per device.

```python
import jax
import jax.numpy as jnp
from jax import lax

D = 1024
HEADS = 16
HEAD_DIM = 64
FF = 4096
MICRO = 2
WIN_T = 5
WIN_S = 8
FRAMES = 10
SPATIAL = 64
OFFSETS = 2025
CLIPS = 16


def draw_frame_counts(key, part):
    clip_total = MICRO * CLIPS
    split_keys = jax.random.split(jax.random.fold_in(key, 17), 4)
    first_draw = jax.random.randint(split_keys[0], (clip_total,), 0, FRAMES - 2)
    second_draw = jax.random.randint(split_keys[1], (clip_total,), 0, FRAMES - 2)
    counts = 2 + jnp.minimum(first_draw, second_draw)
    longest = jax.random.randint(split_keys[2], (), 0, clip_total)
    shortest = (longest + 1 + jax.random.randint(split_keys[3], (), 0, clip_total - 1)) % clip_total
    places = jnp.arange(clip_total)
    counts = jnp.where(places == longest, FRAMES - 1, counts)
    counts = jnp.where(places == shortest, 2, counts)
    return counts.reshape(MICRO, CLIPS).astype(jnp.int32)


def block_levels(rng, extent, shards, smallest, top_value):
    factor_of, own = 1.0, jax.random.fold_in(rng, 6)
    for dim, parts in shards:
        draws = jnp.exp(jax.random.uniform(jax.random.fold_in(own, dim), (parts,), jnp.float32, smallest / len(shards), top_value / len(shards)))
        factor_of = factor_of * jnp.repeat(draws, extent[dim] // parts).reshape([-1 if axis == dim else 1 for axis in range(len(extent))])
    return factor_of


def scatter_about(stream_key, extent, scale, bound, pieces=(), kind=jnp.bfloat16):
    values = jax.random.normal(stream_key, extent, jnp.float32) * scale
    if len(pieces) > 0:
        values = block_levels(stream_key, extent, pieces, -0.22, 0.18) * values
    return jnp.clip(values, min=-bound, max=bound).astype(kind)


def setup_inputs(seed: int = 0) -> dict:
    arg_keys = jax.random.split(jax.random.key(seed), 11)
    return {
        "tokens": scatter_about(arg_keys[0], (MICRO, CLIPS, FRAMES, SPATIAL, D), 1.0, 6.0, ((1, 8), (3, 4))),
        "conditioning": scatter_about(arg_keys[1], (MICRO, CLIPS, D), 1.0, 6.0, ((1, 8),)),
        "frame_counts": draw_frame_counts(jax.random.fold_in(arg_keys[10], 71), 0),
        "w_qkv": scatter_about(arg_keys[3], (D, 3, D), D ** -0.5, 0.1875, ((0, 8), (2, 4))),
        "w_out": scatter_about(arg_keys[4], (D, D), (D // 64) ** -0.5, 1.5, ((0, 8), (1, 4))),
        "w_up": scatter_about(arg_keys[5], (D, FF), D ** -0.5, 0.1875, ((0, 8), (1, 4))),
        "w_down": scatter_about(arg_keys[6], (D, FF), FF ** -0.5, 0.09375, ((0, 8), (1, 4))),
        "w_ada": scatter_about(arg_keys[7], (D, 6 * D), D ** -0.5, 0.1875, ((0, 8), (1, 4))),
        "pos_table": scatter_about(arg_keys[8], (HEADS, OFFSETS), 1.0, 4.0, ((0, 4),), jnp.float32),
        "cotangent": scatter_about(arg_keys[9], (MICRO, CLIPS, FRAMES, SPATIAL, D), 1.0, 6.0, ((1, 8), (3, 4))),
    }


EPSILON = 1e-06
NEGATIVE = -1e+30
HIGHEST = lax.Precision.HIGHEST

@jax.custom_vjp
def low(v):
    return lax.optimization_barrier(v.astype(jnp.bfloat16)).astype(jnp.float32)

@jax.custom_vjp
def low_back(v):
    return v

def low_keep(v):
    return (low(v), None)

def low_pass(kept, grad):
    return (grad,)

def back_keep(v):
    return (v, None)

def back_low(kept, grad):
    return (low(grad),)
low.defvjp(low_keep, low_pass)
low_back.defvjp(back_keep, back_low)

def offset_table():
    length_win = WIN_T * WIN_S * WIN_S
    places = jnp.arange(length_win)
    frame_at = places // (WIN_S * WIN_S)
    row_at = places // WIN_S % WIN_S
    col_at = places % WIN_S
    span_rows = 2 * WIN_S - 1
    index_out = (frame_at[:, None] - frame_at[None, :] + WIN_T - 1) * span_rows * span_rows
    index_out = index_out + (row_at[:, None] - row_at[None, :] + WIN_S - 1) * span_rows
    index_out = index_out + (col_at[:, None] - col_at[None, :] + WIN_S - 1)
    return index_out.astype(jnp.int32)

def ada_norm(values, shift_row, scale_row):
    center = values - lax.optimization_barrier(jnp.mean(values, axis=-1, keepdims=True))
    spread = lax.optimization_barrier(jnp.mean(center * center, axis=-1, keepdims=True))
    return center * lax.rsqrt(spread + EPSILON) * (1.0 + scale_row) + shift_row

def clip_forward(clip_rows, cond_row, count_one, weight_qkv, weight_out, weight_up, weight_down, weight_ada, table_arr):
    window_count = FRAMES // WIN_T
    window_len = WIN_T * SPATIAL
    modulation = jnp.dot(low(jax.nn.silu(cond_row))[None, :], weight_ada, precision=HIGHEST).reshape(6, D)
    frame_live = (jnp.arange(FRAMES) < count_one).astype(jnp.float32)
    token_live = jnp.repeat(frame_live, SPATIAL)
    key_live = token_live.reshape(window_count, window_len)
    flat_rows = clip_rows.reshape(FRAMES * SPATIAL, D)
    normed = low(ada_norm(flat_rows, modulation[0], modulation[1]))
    projected = jnp.einsum('td,dcm->tcm', normed, weight_qkv, precision=HIGHEST)
    projected = low_back(low(projected))
    split_heads = projected.reshape(window_count, window_len, 3, HEADS, HEAD_DIM)
    queries = split_heads[:, :, 0]
    keys_in = split_heads[:, :, 1]
    values_in = split_heads[:, :, 2]
    pos_bias = table_arr[:, offset_table()]
    scores = jnp.einsum('wqhe,wkhe->whqk', queries, keys_in, precision=HIGHEST) * HEAD_DIM ** (-0.5) + pos_bias[None]
    scores = low_back(scores)
    key_mask = key_live[:, None, None, :]
    masked = jnp.where(key_mask > 0, scores, NEGATIVE)
    top_score = lax.optimization_barrier(jnp.max(masked, axis=-1, keepdims=True))
    expo_part = jnp.exp(masked - top_score) * key_mask
    totals = jnp.maximum(lax.optimization_barrier(jnp.sum(expo_part, axis=-1, keepdims=True)), 1.0)
    weights_low = low(expo_part / totals)
    attended = jnp.einsum('whqk,wkhe->wqhe', weights_low, values_in, precision=HIGHEST)
    attended = attended.reshape(FRAMES * SPATIAL, D) * token_live[:, None]
    attended = low_back(low(attended))
    branch_a = low_back(jnp.dot(attended, weight_out.T, precision=HIGHEST))
    middle = flat_rows + modulation[2] * branch_a
    normed_two = low(ada_norm(middle, modulation[3], modulation[4]))
    hidden = low_back(jnp.dot(normed_two, weight_up, precision=HIGHEST))
    activ = low(jax.nn.gelu(hidden))
    branch_b = low_back(jnp.dot(activ, weight_down.T, precision=HIGHEST))
    return (middle + modulation[5] * branch_b).reshape(FRAMES, SPATIAL, D)

def reference(tokens, conditioning, frame_counts, w_qkv, w_out, w_up, w_down, w_ada, pos_table, cotangent):
    clip_total = MICRO * CLIPS
    flat_tokens = tokens.astype(jnp.float32).reshape(clip_total, FRAMES, SPATIAL, D)
    flat_cond = conditioning.astype(jnp.float32).reshape(clip_total, D)
    flat_counts = frame_counts.reshape(clip_total).astype(jnp.int32)

    def forward(token_arr, cond_arr, weight_qkv, weight_out, weight_up, weight_down, weight_ada, table_arr):

        def per_clip(packed):
            return jax.checkpoint(clip_forward)(packed[0], packed[1], packed[2], weight_qkv, weight_out, weight_up, weight_down, weight_ada, table_arr)
        return lax.map(per_clip, (token_arr, cond_arr, flat_counts))
    result, pullback = jax.vjp(forward, flat_tokens, flat_cond, w_qkv.astype(jnp.float32), w_out.astype(jnp.float32), w_up.astype(jnp.float32), w_down.astype(jnp.float32), w_ada.astype(jnp.float32), pos_table.astype(jnp.float32))
    gradients = pullback(cotangent.astype(jnp.float32).reshape(clip_total, FRAMES, SPATIAL, D))
    return (result.reshape(MICRO, CLIPS, FRAMES, SPATIAL, D).astype(jnp.bfloat16), gradients[0].reshape(MICRO, CLIPS, FRAMES, SPATIAL, D).astype(jnp.bfloat16), gradients[1].reshape(MICRO, CLIPS, D), gradients[2], gradients[3], gradients[4], gradients[5], gradients[6], gradients[7])
```

```python
import functools

import jax
import jax.numpy as jnp
import numpy as np
from jax import lax
from jax.experimental import pallas as pl
from jax.experimental.pallas import tpu as pltpu
from jax.sharding import PartitionSpec as P

HEAD_DIM = 64
WIN_T = 5
WIN_S = 8
FRAMES = 10
SPATIAL = 64
OFFSETS = 2025

EPSILON = 1e-06
NEGATIVE = -1e30
HIGHEST = lax.Precision.HIGHEST
BF = jnp.bfloat16
F32 = jnp.float32
WINDOWS = FRAMES // WIN_T
WIN_LEN = WIN_T * SPATIAL
SPREAD = 2 * WIN_T - 1
DIAG = SPREAD * SPATIAL


def stage_bits(n_dp, core):
    bits = list(range(1, n_dp.bit_length() - 1))
    return bits if core == 0 else bits[::-1]


def stage_perm(n_dp, stage):
    return [(i, i ^ (1 << stage_bits(n_dp, i & 1)[stage])) for i in range(n_dp)]


def core_perm(n_dp):
    return [(i, i ^ 1) for i in range(n_dp)]


def ring(count, step):
    return [(i, (i + step) % count) for i in range(count)]


def stages(n_dp):
    return n_dp.bit_length() - 2


def dp_order(n_dp):
    half = n_dp // 2

    def mask(core, place):
        return sum(1 << b for t, b in enumerate(stage_bits(n_dp, core)) if place >> t & 1)

    return np.array(
        [[mask(c, k) for k in range(half)] + [1 ^ mask(1 - c, k) for k in range(half)] for c in (0, 1)],
        np.int32,
    )


def gather_weight(shard, n_dp, n_z):
    blocks = [shard]
    for _ in range(n_z - 1):
        blocks.append(lax.ppermute(blocks[-1], "tensor", ring(n_z, 1)))
    pieces = [jnp.concatenate(blocks, axis=1)]
    for t in range(stages(n_dp)):
        pieces = pieces + [lax.ppermute(p, "dp", stage_perm(n_dp, t)) for p in pieces]
    pieces = pieces + [lax.ppermute(p, "dp", core_perm(n_dp)) for p in pieces]
    return jnp.concatenate(pieces, axis=0)


def add_low(first, second):
    return (first.astype(F32) + second.astype(F32)).astype(BF)


def scatter_grad(grad, n_dp, n_z):
    rows = grad.shape[0] // n_dp
    pieces = [grad[i * rows : (i + 1) * rows] for i in range(n_dp)]
    for t in range(stages(n_dp), -1, -1):
        half = len(pieces) // 2
        perm = core_perm(n_dp) if t == stages(n_dp) else stage_perm(n_dp, t)
        got = [lax.ppermute(p, "dp", perm) for p in pieces[half:]]
        pieces = [add_low(a, b) for a, b in zip(pieces[:half], got)]
    width = grad.shape[1] // n_z
    part = [pieces[0][:, r * width : (r + 1) * width] for r in range(n_z)]
    total = part[n_z - 1]
    for r in range(n_z - 2, -1, -1):
        total = lax.ppermute(total, "tensor", ring(n_z, -1))
        total = add_low(part[r], total) if r else part[r].astype(F32) + total.astype(F32)
    return total


def shifted(pieces, n_z, sign):
    return [pieces[0]] + [lax.ppermute(pieces[r], "tensor", ring(n_z, sign * r)) for r in range(1, n_z)]


def butterfly_sum(value, axis, count):
    bit = 1
    while bit < count:
        value = value + lax.ppermute(value, axis, [(i, i ^ bit) for i in range(count)])
        bit *= 2
    return value


def pair_onehot():
    span = 2 * WIN_S - 1
    place = jnp.arange(SPATIAL)
    row, col = place // WIN_S, place % WIN_S
    offset = (row[:, None] - row[None, :] + WIN_S - 1) * span + (col[:, None] - col[None, :] + WIN_S - 1)
    return (jnp.arange(span * span)[:, None] == offset.reshape(1, -1)).astype(F32)


def spread_bias(table):
    heads = table.shape[0]
    rows = table.reshape(heads, SPREAD, -1)[:, ::-1].reshape(heads * SPREAD, -1)
    flat = jnp.dot(rows, pair_onehot(), precision=HIGHEST)
    flat = flat.reshape(heads, SPREAD, SPATIAL, SPATIAL)
    return flat.transpose(0, 2, 1, 3).reshape(heads, SPATIAL, DIAG)


def fold_bias(diag):
    heads = diag.shape[0]
    rows = diag.reshape(heads, SPATIAL, SPREAD, SPATIAL).transpose(0, 2, 1, 3)
    rows = rows.reshape(heads * SPREAD, SPATIAL * SPATIAL)
    folded = lax.dot_general(rows, pair_onehot(), (((1,), (1,)), ((), ())), precision=HIGHEST)
    return folded.reshape(heads, SPREAD, -1)[:, ::-1].reshape(heads, OFFSETS)


def dot_nt(a, b):
    return lax.dot_general(a, b, (((1,), (1,)), ((), ())), preferred_element_type=F32)


def dot_tn(a, b):
    return lax.dot_general(a, b, (((0,), (0,)), ((), ())), preferred_element_type=F32)


def attend_kernel(heads, count_ref, qkv_ref, bias_ref, att_ref, prob_ref):
    width = heads * HEAD_DIM
    live = (count_ref[0] - pl.program_id(1) * WIN_T) * SPATIAL
    key_live = lax.broadcasted_iota(jnp.int32, (WIN_LEN, WIN_LEN), 1) < live
    row_live = lax.broadcasted_iota(jnp.int32, (WIN_LEN, HEAD_DIM), 0) < live
    for h in range(heads):
        low = h * HEAD_DIM
        q = qkv_ref[:, low : low + HEAD_DIM]
        k = qkv_ref[:, width + low : width + low + HEAD_DIM]
        v = qkv_ref[:, 2 * width + low : 2 * width + low + HEAD_DIM]
        bias = jnp.concatenate(
            [bias_ref[h, :, (WIN_T - 1 - a) * SPATIAL : (WIN_T - 1 - a) * SPATIAL + WIN_LEN] for a in range(WIN_T)],
            axis=0,
        )
        scores = jnp.where(key_live, dot_nt(q, k) * HEAD_DIM**-0.5 + bias, NEGATIVE)
        top = jnp.max(scores, axis=1, keepdims=True)
        expo = jnp.where(key_live, jnp.exp(scores - top), 0.0)
        total = jnp.maximum(jnp.sum(expo, axis=1, keepdims=True), 1.0)
        probs = (expo * (1.0 / total)).astype(BF)
        prob_ref[0, h] = probs
        att = jnp.dot(probs, v, preferred_element_type=F32)
        att_ref[:, low : low + HEAD_DIM] = jnp.where(row_live, att, 0.0).astype(BF)


def attend_back_kernel(heads, count_ref, qkv_ref, prob_ref, gatt_ref, gqkv_ref, diag_ref):
    width = heads * HEAD_DIM
    live = (count_ref[0] - pl.program_id(1) * WIN_T) * SPATIAL
    row_live = lax.broadcasted_iota(jnp.int32, (WIN_LEN, HEAD_DIM), 0) < live

    @pl.when(pl.program_id(1) == 0)
    def _():
        diag_ref[...] = jnp.zeros_like(diag_ref)

    for h in range(heads):
        low = h * HEAD_DIM
        q = qkv_ref[:, low : low + HEAD_DIM]
        k = qkv_ref[:, width + low : width + low + HEAD_DIM]
        v = qkv_ref[:, 2 * width + low : 2 * width + low + HEAD_DIM]
        gatt = gatt_ref[:, low : low + HEAD_DIM]
        gatt = jnp.where(row_live, gatt, jnp.zeros_like(gatt))
        probs = prob_ref[0, h]
        full = probs.astype(F32)
        gvalues = dot_tn(probs, gatt)
        gprobs = dot_nt(gatt, v)
        inner = jnp.sum(full * gprobs, axis=1, keepdims=True)
        gscores = (full * (gprobs - inner)).astype(BF)
        gq = jnp.dot(gscores, k, preferred_element_type=F32) * HEAD_DIM**-0.5
        gk = dot_tn(gscores, q) * HEAD_DIM**-0.5
        gqkv_ref[:, low : low + HEAD_DIM] = gq.astype(BF)
        gqkv_ref[:, width + low : width + low + HEAD_DIM] = gk.astype(BF)
        gqkv_ref[:, 2 * width + low : 2 * width + low + HEAD_DIM] = gvalues.astype(BF)
        wide = gscores.astype(F32)
        for a in range(WIN_T):
            at = (WIN_T - 1 - a) * SPATIAL
            diag_ref[h, :, at : at + WIN_LEN] += wide[a * SPATIAL : (a + 1) * SPATIAL]


def attend(count, qkv, bias, n_z):
    heads = bias.shape[0] // n_z
    width = heads * HEAD_DIM
    return pl.pallas_call(
        functools.partial(attend_kernel, heads),
        grid_spec=pltpu.PrefetchScalarGridSpec(
            num_scalar_prefetch=1,
            grid=(n_z, WINDOWS),
            in_specs=[
                pl.BlockSpec((WIN_LEN, 3 * width), lambda r, w, c: (w, r)),
                pl.BlockSpec((heads, SPATIAL, DIAG), lambda r, w, c: (r, 0, 0)),
            ],
            out_specs=[
                pl.BlockSpec((WIN_LEN, width), lambda r, w, c: (w, r)),
                pl.BlockSpec((1, heads, WIN_LEN, WIN_LEN), lambda r, w, c: (w, r, 0, 0)),
            ],
        ),
        out_shape=[
            jax.ShapeDtypeStruct((WINDOWS * WIN_LEN, n_z * width), BF),
            jax.ShapeDtypeStruct((WINDOWS, n_z * heads, WIN_LEN, WIN_LEN), BF),
        ],
        compiler_params=pltpu.CompilerParams(vmem_limit_bytes=32 << 20),
        cost_estimate=pl.CostEstimate(flops=2 * 10**9, bytes_accessed=14 * 10**6, transcendentals=3 * 10**6),
        name="attend",
    )(count, qkv, bias)


def attend_back(count, qkv, probs, gatt, n_z):
    heads = probs.shape[1] // n_z
    width = heads * HEAD_DIM
    return pl.pallas_call(
        functools.partial(attend_back_kernel, heads),
        grid_spec=pltpu.PrefetchScalarGridSpec(
            num_scalar_prefetch=1,
            grid=(n_z, WINDOWS),
            in_specs=[
                pl.BlockSpec((WIN_LEN, 3 * width), lambda r, w, c: (w, r)),
                pl.BlockSpec((1, heads, WIN_LEN, WIN_LEN), lambda r, w, c: (w, r, 0, 0)),
                pl.BlockSpec((WIN_LEN, width), lambda r, w, c: (w, r)),
            ],
            out_specs=[
                pl.BlockSpec((WIN_LEN, 3 * width), lambda r, w, c: (w, r)),
                pl.BlockSpec((heads, SPATIAL, DIAG), lambda r, w, c: (r, 0, 0)),
            ],
        ),
        out_shape=[
            jax.ShapeDtypeStruct((WINDOWS * WIN_LEN, n_z * 3 * width), BF),
            jax.ShapeDtypeStruct((n_z * heads, SPATIAL, DIAG), F32),
        ],
        compiler_params=pltpu.CompilerParams(vmem_limit_bytes=32 << 20),
        cost_estimate=pl.CostEstimate(flops=5 * 10**9, bytes_accessed=18 * 10**6, transcendentals=0),
        name="attend_back",
    )(count, qkv, probs, gatt)


def normalize(values):
    center = values - jnp.mean(values, axis=-1, keepdims=True)
    scale = lax.rsqrt(jnp.mean(center * center, axis=-1, keepdims=True) + EPSILON)
    return center * scale, scale


def norm_back(normed, inv_sigma, scale_row, grad):
    u = (1.0 + scale_row) * grad
    return (u - jnp.mean(u, axis=-1, keepdims=True) - normed * jnp.mean(u * normed, axis=-1, keepdims=True)) * inv_sigma


def gelu_slope(v):
    c = np.float32(np.sqrt(2 / np.pi))
    t = jnp.tanh(c * (v + 0.044715 * v * v * v))
    return 0.5 * (1.0 + t) + 0.5 * v * (1.0 - t * t) * c * (1.0 + 3 * 0.044715 * v * v)


def dot(a, b):
    return jnp.dot(a, b, preferred_element_type=F32)


def body(
    n_dp, n_z, tokens, conditioning, frame_counts, w_qkv, w_out, w_up, w_down, w_ada, pos_table, cotangent
):
    micro, clip_dev, _, part, model = tokens.shape
    clips = micro * clip_dev
    assert clips == n_z and part * n_z == SPATIAL
    feature = model // n_dp
    d, z = lax.axis_index("dp"), lax.axis_index("tensor")
    count = lax.dynamic_slice_in_dim(frame_counts.reshape(clips), z, 1)

    order = jnp.asarray(dp_order(n_dp))[d & 1] ^ d
    source = (order[:, None] * feature + jnp.arange(feature)[None, :]).reshape(1, model)
    to_place = (jnp.arange(model)[:, None] == source).astype(BF)

    def placed(rows):
        return dot(rows, to_place).astype(BF)

    def unplaced(rows):
        return dot_nt(rows.astype(BF), to_place).astype(BF)

    def to_clip(rows):
        got = lax.all_to_all(rows.reshape(clips, FRAMES, part, model), "tensor", 0, 0, tiled=True)
        return got.transpose(1, 0, 2, 3).reshape(FRAMES * SPATIAL, model)

    def from_clip(rows):
        parts = rows.reshape(FRAMES, n_z, part, model).transpose(1, 0, 2, 3)
        return lax.all_to_all(parts, "tensor", 0, 0, tiled=True).reshape(tokens.shape)

    cond_float = conditioning.astype(F32).reshape(clips, model)
    cond_act = jax.nn.silu(cond_float).astype(BF)
    cond_mine = lax.all_to_all(
        cond_act.reshape(clips, n_dp, feature).transpose(1, 0, 2), "dp", 0, 0, tiled=True
    ).reshape(n_dp * clips, feature)
    mod_part = lax.all_to_all(dot(cond_mine, w_ada), ("dp", "tensor"), 0, 0, tiled=True)
    mods = jnp.sum(mod_part.reshape(n_dp, n_z, -1), axis=0).reshape(6, model)
    mods = jnp.dot(mods, to_place.astype(F32), precision=HIGHEST).reshape(6, 1, model)

    wq = gather_weight(w_qkv.reshape(feature, -1), n_dp, n_z)
    wo = gather_weight(w_out, n_dp, n_z)
    wu = gather_weight(w_up, n_dp, n_z)
    wd = gather_weight(w_down, n_dp, n_z)

    bias = spread_bias(jnp.concatenate(shifted([pos_table] * n_z, n_z, 1), axis=0))

    resid = placed(to_clip(tokens)).astype(F32)
    norm_a, inv_a = normalize(resid)
    normed_a = (norm_a * (1.0 + mods[1]) + mods[0]).astype(BF)
    qkv = dot(normed_a, wq).astype(BF)
    attended, probs = attend(count, qkv, bias, n_z)
    branch_a = dot_nt(attended, wo)
    middle = resid + mods[2] * branch_a
    norm_b, inv_b = normalize(middle)
    normed_b = (norm_b * (1.0 + mods[4]) + mods[3]).astype(BF)
    hidden = dot(normed_b, wu)
    activ = jax.nn.gelu(hidden).astype(BF)
    slope = gelu_slope(hidden).astype(BF)
    grad_result = placed(to_clip(cotangent)).astype(F32)
    grad_bb = (grad_result * mods[5]).astype(BF)
    grad_down = dot_tn(grad_bb, activ).astype(BF)
    out_down = scatter_grad(grad_down, n_dp, n_z)
    branch_b = dot_nt(activ, wd)
    block_out = from_clip(unplaced(middle + mods[5] * branch_b))

    grad_gate_b = jnp.sum(grad_result * branch_b, axis=0)
    grad_hidden = (dot(grad_bb, wd) * slope.astype(F32)).astype(BF)
    grad_up = dot_tn(normed_b, grad_hidden).astype(BF)
    out_up = scatter_grad(grad_up, n_dp, n_z)
    grad_nb = dot_nt(grad_hidden, wu)
    grad_shift_b = jnp.sum(grad_nb, axis=0)
    grad_scale_b = jnp.sum(grad_nb * norm_b, axis=0)
    grad_middle = grad_result + norm_back(norm_b, inv_b, mods[4], grad_nb)
    grad_ba = (grad_middle * mods[2]).astype(BF)
    grad_gate_a = jnp.sum(grad_middle * branch_a, axis=0)
    grad_out = dot_tn(grad_ba, attended).astype(BF)
    out_out = scatter_grad(grad_out, n_dp, n_z)
    grad_att = dot(grad_ba, wo).astype(BF)
    grad_qkv, diag = attend_back(count, qkv, probs, grad_att, n_z)
    grad_in = dot_tn(normed_a, grad_qkv).astype(BF)
    out_qkv = scatter_grad(grad_in, n_dp, n_z)
    grad_na = dot_nt(grad_qkv, wq)
    grad_shift_a = jnp.sum(grad_na, axis=0)
    grad_scale_a = jnp.sum(grad_na * norm_a, axis=0)
    grad_tokens = from_clip(unplaced(grad_middle + norm_back(norm_a, inv_a, mods[1], grad_na)))

    table = fold_bias(diag)
    heads = table.shape[0] // n_z
    own = shifted([table[r * heads : (r + 1) * heads] for r in range(n_z)], n_z, -1)
    grad_table = butterfly_sum(functools.reduce(lambda a, b: a + b, own), "dp", n_dp)

    grad_mod = jnp.stack([grad_shift_a, grad_scale_a, grad_gate_a, grad_shift_b, grad_scale_b, grad_gate_b])
    grad_mod = unplaced(grad_mod).reshape(1, n_z, -1)
    grad_mod = jnp.broadcast_to(grad_mod, (n_dp,) + grad_mod.shape[1:]).reshape(n_dp * n_z, -1)
    mod_cols = lax.all_to_all(grad_mod, ("dp", "tensor"), 0, 0, tiled=True)
    grad_ada = dot_tn(cond_mine, mod_cols)
    act_part = dot_nt(mod_cols, w_ada).reshape(n_dp, clips, feature)
    act_part = lax.all_to_all(act_part, "dp", 0, 0, tiled=True)
    grad_act = butterfly_sum(act_part, "tensor", n_z).transpose(1, 0, 2).reshape(clips, model)
    grad_cond = jax.vjp(jax.nn.silu, cond_float)[1](grad_act)[0].reshape(conditioning.shape)
    return (
        block_out,
        grad_tokens,
        grad_cond,
        out_qkv.reshape(w_qkv.shape),
        out_out,
        out_up,
        out_down,
        grad_ada,
        grad_table,
    )


def solution(mesh):
    rows = P(None, "dp", None, "tensor", None)
    weight = P("dp", "tensor")
    qkv_weight = P("dp", None, "tensor")
    cond = P(None, "dp", None)
    table = P("tensor", None)
    return jax.shard_map(
        functools.partial(body, mesh.shape["dp"], mesh.shape["tensor"]),
        mesh=mesh,
        in_specs=(rows, cond, P(None, "dp"), qkv_weight, weight, weight, weight, weight, table, rows),
        out_specs=(rows, rows, cond, qkv_weight, weight, weight, weight, weight, table),
        check_vma=False,
    )
```

```python
import functools

import jax
import jax.numpy as jnp
import numpy as np
from jax import lax
from jax.experimental import pallas as pl
from jax.experimental.pallas import tpu as pltpu
from jax.sharding import PartitionSpec as P

HEAD_DIM = 64
WIN_T = 5
WIN_S = 8
FRAMES = 10
SPATIAL = 64
OFFSETS = 2025

EPSILON = 1e-06
NEGATIVE = -1e30
HIGHEST = lax.Precision.HIGHEST
BF = jnp.bfloat16
F32 = jnp.float32
WINDOWS = FRAMES // WIN_T
WIN_LEN = WIN_T * SPATIAL
SPREAD = 2 * WIN_T - 1
DIAG = SPREAD * SPATIAL
GROUPS = 4
VMEM = 56 << 20


def stage_bits(n_dp, core):
    bits = list(range(1, n_dp.bit_length() - 1))
    return bits if core == 0 else bits[::-1]


def stage_perm(n_dp, stage):
    return [(i, i ^ (1 << stage_bits(n_dp, i & 1)[stage])) for i in range(n_dp)]


def core_perm(n_dp):
    return [(i, i ^ 1) for i in range(n_dp)]


def ring(count, step):
    return [(i, (i + step) % count) for i in range(count)]


def stages(n_dp):
    return n_dp.bit_length() - 2


def dp_order(n_dp):
    half = n_dp // 2

    def mask(core, place):
        return sum(1 << b for t, b in enumerate(stage_bits(n_dp, core)) if place >> t & 1)

    return np.array(
        [[mask(c, k) for k in range(half)] + [1 ^ mask(1 - c, k) for k in range(half)] for c in (0, 1)],
        np.int32,
    )


def merged(pieces):
    if len(pieces) <= GROUPS:
        return pieces
    return [jnp.concatenate(pieces[i : i + 2], axis=0) for i in range(0, len(pieces), 2)]


def gather_steps(n_dp, n_z, shard, direct):
    blocks = [shard]
    if direct:
        blocks = yield shifted([shard] * n_z, n_z, 1)
    else:
        for _ in range(n_z - 1):
            blocks = yield blocks + [lax.ppermute(blocks[-1], "tensor", ring(n_z, 1))]
    pieces = [jnp.concatenate(blocks, axis=1)]
    for t in range(stages(n_dp)):
        perm = stage_perm(n_dp, t)
        pieces = yield merged(pieces + [lax.ppermute(p, "dp", perm) for p in pieces])
    yield pieces + [lax.ppermute(p, "dp", core_perm(n_dp)) for p in pieces]


def add_low(first, second):
    return (first.astype(F32) + second.astype(F32)).astype(BF)


def scatter_steps(n_dp, n_z, halves, direct):
    keep, send = halves
    for t in range(stages(n_dp), -1, -1):
        perm = core_perm(n_dp) if t == stages(n_dp) else stage_perm(n_dp, t)
        got = lax.ppermute(send, "dp", perm)
        if t:
            rows = keep.shape[0] // 2
            keep, send = yield add_low(keep[:rows], got[:rows]), add_low(keep[rows:], got[rows:])
    width = keep.shape[1] // n_z
    part = [add_low(keep[:, r * width : (r + 1) * width], got[:, r * width : (r + 1) * width]) for r in range(n_z)]
    part = yield part
    if direct:
        yield functools.reduce(lambda a, b: a + b, [p.astype(F32) for p in shifted(part, n_z, -1)])
        return
    for r in range(n_z - 2, -1, -1):
        total = lax.ppermute(part[r + 1], "tensor", ring(n_z, -1))
        if r:
            part = yield part[:r] + [add_low(part[r], total)]
        else:
            yield part[0].astype(F32) + total.astype(F32)


class Chain:
    def __init__(self, name, steps, total):
        self.name, self.steps, self.left, self.value = name, steps, total, None

    def step(self):
        with jax.named_scope(f"{self.name}_{self.left}_left"):
            self.value = self.steps.send(self.value)
        self.left -= 1


def slot(chains, *values, free=()):
    chains = [c for c in chains if c.left]
    for chain in chains + [c for c in free if c.left]:
        chain.step()
    held, values = lax.optimization_barrier(([c.value for c in chains], values))
    for chain, value in zip(chains, held):
        chain.value = value
    return values[0] if len(values) == 1 else values


def whole(chain):
    while chain.left:
        slot([chain])
    return chain.value


def shifted(pieces, n_z, sign):
    return [pieces[0]] + [lax.ppermute(pieces[r], "tensor", ring(n_z, sign * r)) for r in range(1, n_z)]


def exchange_steps(pieces, n_z, sign):
    pieces = list(pieces)
    for group in ([n_z // 2], [r for r in range(1, n_z) if r != n_z // 2]):
        for r in group:
            pieces[r] = lax.ppermute(pieces[r], "tensor", ring(n_z, sign * r))
        pieces = yield pieces


def butterfly_steps(value, axis, count):
    bit = 1
    while bit < count:
        value = yield value + lax.ppermute(value, axis, [(i, i ^ bit) for i in range(count)])
        bit *= 2


def pair_onehot(place):
    span = 2 * WIN_S - 1
    row, col = place // WIN_S, place % WIN_S
    offset = (row[None, :] - row[:, None] + WIN_S - 1) * span + (col[None, :] - col[:, None] + WIN_S - 1)
    return (jnp.arange(span * span)[:, None] == offset.reshape(1, -1)).astype(F32)


def spread_bias(table, place):
    heads = table.shape[0]
    flat = jnp.dot(table.reshape(heads * SPREAD, -1), pair_onehot(place), precision=HIGHEST)
    return flat.reshape(heads, SPREAD, SPATIAL, SPATIAL)


def fold_bias(diag, place):
    heads = diag.shape[0]
    rows = diag.reshape(heads * SPREAD, SPATIAL * SPATIAL)
    folded = lax.dot_general(rows, pair_onehot(place), (((1,), (1,)), ((), ())), precision=HIGHEST)
    return folded.reshape(heads, OFFSETS)


def dot(a, b):
    return jnp.dot(a, b, preferred_element_type=F32)


def dot_nt(a, b):
    return lax.dot_general(a, b, (((1,), (1,)), ((), ())), preferred_element_type=F32)


def dot_tn(a, b):
    return lax.dot_general(a, b, (((0,), (0,)), ((), ())), preferred_element_type=F32)


def params():
    return pltpu.CompilerParams(vmem_limit_bytes=VMEM)


COST = pl.CostEstimate(flops=10**6, bytes_accessed=10**4, transcendentals=0)


class Pieces:
    def __init__(self, pieces, width, take, at):
        self.many, self.pieces = len(at(0)), len(pieces)
        self.arrays = [p for p in pieces for _ in range(self.many)]
        self.width, self.take, self.at = width, take, at
        self.rows = sum(p.shape[0] for p in pieces)

    def specs(self):
        return [
            pl.BlockSpec((a.shape[0], self.width), lambda j, p, i=i % self.many: (0, self.at(j)[i]))
            for i, a in enumerate(self.arrays)
        ]

    def load(self, refs, places):
        rows = [
            jnp.concatenate([r[:, : self.take] for r in refs[i : i + self.many]], axis=1)
            for i in range(0, len(refs), self.many)
        ]
        return jnp.concatenate(rows, axis=0)


class Gathered:
    def __init__(self, array):
        self.arrays = [array]
        self.count, self.width = array.shape[0], array.shape[3]
        self.rows = array.shape[0] * array.shape[2]

    def specs(self):
        n_dp, _, rows, columns = self.arrays[0].shape
        return [pl.BlockSpec((n_dp, 1, rows, columns), lambda j, p: (0, p[n_dp + j], 0, 0))]

    def load(self, refs, places):
        return jnp.concatenate([refs[0][places[k], 0] for k in range(self.count)], axis=0)


def rows_times(places, x, weight, columns, tile, finish, extra, outs, name):
    length, depth = x.shape
    count = len(weight.arrays)

    def kernel(places_ref, x_ref, *refs):
        w = weight.load(refs[:count], places_ref)
        done = finish(dot(x_ref[...], w), *(r[...] for r in refs[count : count + len(extra)]))
        for ref, value in zip(refs[count + len(extra) :], done):
            ref[...] = value

    tall = pl.BlockSpec((length, tile), lambda j, p: (0, j))
    return pl.pallas_call(
        kernel,
        grid_spec=pltpu.PrefetchScalarGridSpec(
            num_scalar_prefetch=1,
            grid=(columns // tile,),
            in_specs=[pl.BlockSpec((length, depth), lambda j, p: (0, 0))] + weight.specs() + [tall] * len(extra),
            out_specs=[tall] * len(outs),
        ),
        out_shape=[jax.ShapeDtypeStruct((length, columns), t) for t in outs],
        compiler_params=params(),
        cost_estimate=COST,
        name=name,
    )(places, x, *weight.arrays, *extra)


def rows_times_t(places, x, weight, tile, name):
    length, depth = x.shape
    count = len(weight.arrays)

    def kernel(places_ref, x_ref, *refs):
        term = dot_nt(x_ref[...], weight.load(refs[:count], places_ref))

        @pl.when(pl.program_id(0) == 0)
        def _():
            refs[count][...] = term

        @pl.when(pl.program_id(0) > 0)
        def _():
            refs[count][...] += term

    return pl.pallas_call(
        kernel,
        grid_spec=pltpu.PrefetchScalarGridSpec(
            num_scalar_prefetch=1,
            grid=(depth // tile,),
            in_specs=[pl.BlockSpec((length, tile), lambda j, p: (0, j))] + weight.specs(),
            out_specs=pl.BlockSpec((length, weight.rows), lambda j, p: (0, 0)),
        ),
        out_shape=jax.ShapeDtypeStruct((length, weight.rows), F32),
        compiler_params=params(),
        cost_estimate=COST,
        name=name,
    )(places, x, *weight.arrays)


def rows_against(x, y, tile, name, places=None, n_dp=1):
    length, depth = x.shape
    columns = y.shape[1]
    rows = depth // n_dp

    def kernel(places_ref, x_ref, y_ref, *refs):
        turned = refs[-1]

        @pl.when(pl.program_id(0) == 0)
        def _():
            turned[...] = x_ref[...].T

        result = dot(turned[...], y_ref[...]).astype(BF)
        if n_dp == 1:
            refs[0][...] = result[: depth // 2]
            refs[1][...] = result[depth // 2 :]
        else:
            for k in range(n_dp):
                refs[0][places_ref[k]] = result[k * rows : (k + 1) * rows]

    if n_dp == 1:
        shape = jax.ShapeDtypeStruct((depth // 2, columns), BF)
        half = pl.BlockSpec((depth // 2, tile), lambda j, p: (0, j))
        out_shape, out_specs = [shape, shape], [half, half]
        places = jnp.zeros((1,), jnp.int32)
    else:
        out_shape = jax.ShapeDtypeStruct((n_dp, rows, columns), BF)
        out_specs = pl.BlockSpec((n_dp, rows, tile), lambda j, p: (0, 0, j))
    return pl.pallas_call(
        kernel,
        grid_spec=pltpu.PrefetchScalarGridSpec(
            num_scalar_prefetch=1,
            grid=(columns // tile,),
            in_specs=[
                pl.BlockSpec((length, depth), lambda j, p: (0, 0)),
                pl.BlockSpec((length, tile), lambda j, p: (0, j)),
            ],
            out_specs=out_specs,
            scratch_shapes=[pltpu.VMEM((depth, length), BF)],
        ),
        out_shape=out_shape,
        compiler_params=params(),
        cost_estimate=COST,
        name=name,
    )(places, x, y)


def head_cols(kind, h, width):
    return slice(kind * width + h * HEAD_DIM, kind * width + (h + 1) * HEAD_DIM)


def attend_kernel(heads, count_ref, qkv_ref, bias_ref, att_ref, prob_ref):
    width = heads * HEAD_DIM
    scale = jnp.asarray(HEAD_DIM**-0.5, BF)
    key_at = lax.broadcasted_iota(jnp.int32, (WIN_LEN, WIN_LEN), 0)
    row_at = lax.broadcasted_iota(jnp.int32, (WIN_LEN, width), 0)
    att = [[] for _ in range(WINDOWS)]
    for h in range(heads):
        bias = jnp.concatenate(
            [
                jnp.concatenate([bias_ref[h, a - b + WIN_T - 1] for a in range(WIN_T)], axis=1)
                for b in range(WIN_T)
            ],
            axis=0,
        )
        for w in range(WINDOWS):
            live = (count_ref[0] - w * WIN_T) * SPATIAL
            rows = slice(w * WIN_LEN, (w + 1) * WIN_LEN)
            q = qkv_ref[rows, head_cols(0, h, width)] * scale
            k = qkv_ref[rows, head_cols(1, h, width)]
            v = qkv_ref[rows, head_cols(2, h, width)]
            scores = jnp.where(key_at < live, dot_nt(k, q) + bias, NEGATIVE)
            top = jnp.max(scores, axis=0, keepdims=True)
            expo = jnp.exp(scores - top)
            total = jnp.maximum(jnp.sum(expo, axis=0, keepdims=True), 1.0)
            probs = (expo * jnp.where(live > 0, 1.0 / total, 0.0)).astype(BF)
            prob_ref[w, h] = probs
            att[w].append(dot_tn(v, probs))
    for w in range(WINDOWS):
        live = (count_ref[0] - w * WIN_T) * SPATIAL
        whole = jnp.concatenate(att[w], axis=0).T
        att_ref[w * WIN_LEN : (w + 1) * WIN_LEN, :] = jnp.where(row_at < live, whole, 0.0).astype(BF)


def attend_back_kernel(heads, count_ref, qkv_ref, prob_ref, gatt_ref, gqkv_ref, diag_ref):
    width = heads * HEAD_DIM
    scale = jnp.asarray(HEAD_DIM**-0.5, BF)
    row_at = lax.broadcasted_iota(jnp.int32, (WIN_LEN, HEAD_DIM), 0)
    grad_q = [[] for _ in range(WINDOWS)]
    for h in range(heads):
        both = None
        for w in range(WINDOWS):
            live = (count_ref[0] - w * WIN_T) * SPATIAL
            rows = slice(w * WIN_LEN, (w + 1) * WIN_LEN)
            q = qkv_ref[rows, head_cols(0, h, width)] * scale
            k = qkv_ref[rows, head_cols(1, h, width)] * scale
            v = qkv_ref[rows, head_cols(2, h, width)]
            gatt = gatt_ref[rows, head_cols(0, h, width)]
            gatt = jnp.where(row_at < live, gatt, jnp.zeros_like(gatt))
            probs = prob_ref[w, h]
            full = probs.astype(F32)
            gqkv_ref[rows, head_cols(2, h, width)] = dot(probs, gatt).astype(BF)
            gprobs = dot_nt(v, gatt)
            inner = jnp.sum(full * gprobs, axis=0, keepdims=True)
            gscores = (full * (gprobs - inner)).astype(BF)
            gqkv_ref[rows, head_cols(1, h, width)] = dot(gscores, q).astype(BF)
            grad_q[w].append(dot_tn(k, gscores))
            wide = gscores.astype(F32)
            both = wide if both is None else both + wide
        blocks = [both[b * SPATIAL : (b + 1) * SPATIAL] for b in range(WIN_T)]
        for t in range(SPREAD):
            pairs = [(b, b + t - WIN_T + 1) for b in range(WIN_T) if 0 <= b + t - WIN_T + 1 < WIN_T]
            diag_ref[h, t] = functools.reduce(
                lambda x, y: x + y, [blocks[b][:, a * SPATIAL : (a + 1) * SPATIAL] for b, a in pairs]
            )
    for w in range(WINDOWS):
        whole = jnp.concatenate(grad_q[w], axis=0).T
        gqkv_ref[w * WIN_LEN : (w + 1) * WIN_LEN, 0:width] = whole.astype(BF)


def attend(count, qkv, bias, n_z):
    heads = bias.shape[0] // n_z
    width = heads * HEAD_DIM
    length = WINDOWS * WIN_LEN
    return pl.pallas_call(
        functools.partial(attend_kernel, heads),
        grid_spec=pltpu.PrefetchScalarGridSpec(
            num_scalar_prefetch=1,
            grid=(n_z,),
            in_specs=[
                pl.BlockSpec((length, 3 * width), lambda r, c: (0, r)),
                pl.BlockSpec((heads, SPREAD, SPATIAL, SPATIAL), lambda r, c: (r, 0, 0, 0)),
            ],
            out_specs=[
                pl.BlockSpec((length, width), lambda r, c: (0, r)),
                pl.BlockSpec((WINDOWS, heads, WIN_LEN, WIN_LEN), lambda r, c: (0, r, 0, 0)),
            ],
        ),
        out_shape=[
            jax.ShapeDtypeStruct((length, n_z * width), BF),
            jax.ShapeDtypeStruct((WINDOWS, n_z * heads, WIN_LEN, WIN_LEN), BF),
        ],
        compiler_params=params(),
        cost_estimate=COST,
        name="attend",
    )(count, qkv, bias)


def attend_back(count, qkv, probs, gatt, n_z):
    heads = probs.shape[1] // n_z
    width = heads * HEAD_DIM
    length = WINDOWS * WIN_LEN
    return pl.pallas_call(
        functools.partial(attend_back_kernel, heads),
        grid_spec=pltpu.PrefetchScalarGridSpec(
            num_scalar_prefetch=1,
            grid=(n_z,),
            in_specs=[
                pl.BlockSpec((length, 3 * width), lambda r, c: (0, r)),
                pl.BlockSpec((WINDOWS, heads, WIN_LEN, WIN_LEN), lambda r, c: (0, r, 0, 0)),
                pl.BlockSpec((length, width), lambda r, c: (0, r)),
            ],
            out_specs=[
                pl.BlockSpec((length, 3 * width), lambda r, c: (0, r)),
                pl.BlockSpec((heads, SPREAD, SPATIAL, SPATIAL), lambda r, c: (r, 0, 0, 0)),
            ],
        ),
        out_shape=[
            jax.ShapeDtypeStruct((length, n_z * 3 * width), BF),
            jax.ShapeDtypeStruct((n_z * heads, SPREAD, SPATIAL, SPATIAL), F32),
        ],
        compiler_params=params(),
        cost_estimate=COST,
        name="attend_back",
    )(count, qkv, probs, gatt)


def normalize(values):
    center = values - jnp.mean(values, axis=-1, keepdims=True)
    scale = lax.rsqrt(jnp.mean(center * center, axis=-1, keepdims=True) + EPSILON)
    return center * scale, scale


def norm_back(normed, inv_sigma, scale_row, grad):
    u = (1.0 + scale_row) * grad
    return (u - jnp.mean(u, axis=-1, keepdims=True) - normed * jnp.mean(u * normed, axis=-1, keepdims=True)) * inv_sigma


def gelu_and_slope(v):
    c = float(np.sqrt(2 / np.pi))
    square = v * v
    h = 0.5 + 0.5 * jnp.tanh(v * (c + (0.044715 * c) * square))
    slope = h + h * (1.0 - h) * (v * (2 * c + (6 * 0.044715 * c) * square))
    return (v * h).astype(BF), slope.astype(BF)


def body(
    n_dp, n_z, tokens, conditioning, frame_counts, w_qkv, w_out, w_up, w_down, w_ada, pos_table, cotangent
):
    micro, clip_dev, _, part, model = tokens.shape
    clips = micro * clip_dev
    assert clips == n_z and part * n_z == SPATIAL
    feature = model // n_dp
    qkv_tile, hidden_tile, out_tile = 3 * w_out.shape[1], w_up.shape[1], w_out.shape[1]
    d, z = lax.axis_index("dp"), lax.axis_index("tensor")
    count = lax.dynamic_slice_in_dim(frame_counts.reshape(clips), z, 1)

    order = jnp.asarray(dp_order(n_dp))[d & 1] ^ d
    source = (order[:, None] * feature + jnp.arange(feature)[None, :]).reshape(1, model)
    to_place = (jnp.arange(model)[:, None] == source).astype(BF)

    places = jnp.concatenate([order, (z - jnp.arange(n_z)) % n_z]).astype(jnp.int32)

    def placed(rows):
        return dot(rows, to_place).astype(BF)

    def unplaced(rows):
        return dot_nt(rows.astype(BF), to_place).astype(BF)

    place = jnp.arange(SPATIAL)
    place = (z - place // part) % n_z * part + place % part

    def for_clips(rows):
        rows = rows.reshape(clips, FRAMES, part, model)
        return [lax.dynamic_index_in_dim(rows, (z + r) % n_z, 0, False) for r in range(n_z)]

    def to_clip(parts):
        with jax.named_scope("tokens_in"):
            return shifted(parts, n_z, 1)

    def in_order(got):
        return placed(jnp.stack(got, axis=1).reshape(FRAMES * SPATIAL, model)).astype(F32)

    def from_clip(rows):
        rows = rows.reshape(FRAMES, n_z, part, model)
        return [rows[:, r] for r in range(n_z)]

    def by_clip(got):
        whole_rows = jnp.zeros((clips, FRAMES, part, model), BF)
        for r in range(n_z):
            whole_rows = lax.dynamic_update_index_in_dim(whole_rows, got[r], (z + r) % n_z, 0)
        return whole_rows.reshape(tokens.shape)

    def gather(name, shard, direct=True):
        return Chain("gather_" + name, gather_steps(n_dp, n_z, shard, direct), stages(n_dp) + (2 if direct else n_z))

    def scatter(name, halves, direct=True):
        return Chain("scatter_" + name, scatter_steps(n_dp, n_z, halves, direct), stages(n_dp) + (2 if direct else n_z))

    def sum_dp(name, halves):
        return Chain("scatter_" + name, scatter_steps(n_dp, n_z, halves, True), stages(n_dp) + 1)

    def exchange(name, pieces, sign):
        return Chain(name, exchange_steps(pieces, n_z, sign), 2)

    def butterfly(name, value, axis, size):
        return Chain(name, butterfly_steps(value, axis, size), size.bit_length() - 1)

    both = jnp.concatenate([w_qkv.reshape(feature, -1), w_out], axis=1)
    per_tile = both.shape[1] // out_tile
    wa = gather("attention", both)

    cond_float = conditioning.astype(F32).reshape(clips, model)
    cond_act = jax.nn.silu(cond_float).astype(BF)
    cond_mine = lax.all_to_all(
        cond_act.reshape(clips, n_dp, feature).transpose(1, 0, 2), "dp", 0, 0, tiled=True
    ).reshape(n_dp * clips, feature)
    mod_part = lax.all_to_all(dot(cond_mine, w_ada), ("dp", "tensor"), 0, 0, tiled=True)
    to_place, got_tokens, pos_table, places, count, mod_part = slot(
        [wa], to_place, for_clips(tokens), pos_table, places, count, mod_part
    )
    table = lax.all_to_all(jnp.broadcast_to(pos_table, (n_z,) + pos_table.shape), "tensor", 0, 0, tiled=True)
    mods = jnp.sum(mod_part.reshape(n_dp, n_z, -1), axis=0).reshape(6, model)
    mods = jnp.dot(mods, to_place.astype(F32), precision=HIGHEST).reshape(6, 1, model)
    got_tokens, table, mods, w_up = slot([wa], to_clip(got_tokens), table, mods, w_up)
    wu = Gathered(lax.all_gather(w_up, ("dp", "tensor"), axis=0).reshape(n_dp, n_z, feature, -1))
    resid = in_order(got_tokens)
    norm_a, inv_a = normalize(resid)
    normed_a = (norm_a * (1.0 + mods[1]) + mods[0]).astype(BF)
    normed_a, w_down = lax.optimization_barrier((normed_a, w_down))
    wd = gather("down", w_down)
    table = table[::-1]
    table = lax.dynamic_slice_in_dim(jnp.concatenate([table, table], axis=0), n_z - 1 - z, n_z, axis=0)
    bias = spread_bias(table.reshape(-1, OFFSETS), place)
    bias, normed_a, cotangent = slot([wa, wd], bias, normed_a, for_clips(cotangent))
    normed_a = slot([wa], normed_a)

    w_in = Pieces(whole(wa), both.shape[1], qkv_tile, lambda j: [j])
    w_mix = Pieces(wa.value, out_tile, out_tile, lambda j: [(2 * j + i) * per_tile + per_tile - 1 for i in (0, 1)])
    qkv, = rows_times(places, normed_a, w_in, qkv_tile * n_z, qkv_tile, lambda v: (v.astype(BF),), (), (BF,), "qkv")
    attended, probs = attend(count, qkv, bias, n_z)
    attended, probs, got_cotangent = slot([], attended, probs, to_clip(cotangent))
    branch_a = rows_times_t(places, attended, w_mix, 2 * out_tile, "out")
    middle = resid + mods[2] * branch_a
    norm_b, inv_b = normalize(middle)
    normed_b = (norm_b * (1.0 + mods[4]) + mods[3]).astype(BF)
    normed_b, got_cotangent = slot([wd], normed_b, got_cotangent)
    activ, slope = rows_times(places, normed_b, wu, hidden_tile * n_z, hidden_tile, gelu_and_slope, (), (BF, BF), "up")
    grad_result = in_order(got_cotangent)
    grad_bb = (grad_result * mods[5]).astype(BF)
    gd = rows_against(grad_bb, activ, hidden_tile, "grad_down")
    activ, slope, grad_bb, gd = slot([wd], activ, slope, grad_bb, gd)
    gd = scatter("down", gd)
    activ, slope, grad_bb = slot([wd, gd], activ, slope, grad_bb)

    wd = Pieces(whole(wd), hidden_tile, hidden_tile, lambda j: [j])
    grad_hidden, = rows_times(
        places, grad_bb, wd, hidden_tile * n_z, hidden_tile, lambda v, s: ((v * s.astype(F32)).astype(BF),), (slope,), (BF,),
        "grad_hidden",
    )
    gu = rows_against(normed_b, grad_hidden, hidden_tile, "grad_up", places, n_dp)
    grad_hidden, gu, activ = slot([gd], grad_hidden, gu, activ)
    gu = lax.psum_scatter(gu.reshape(model, -1), "dp", scatter_dimension=0, tiled=True)
    grad_nb = rows_times_t(places, grad_hidden, wu, hidden_tile, "grad_normed_b")
    branch_b = rows_times_t(places, activ, wd, hidden_tile, "down")
    grad_nb, branch_b = slot([gd], grad_nb, branch_b)
    grad_middle = grad_result + norm_back(norm_b, inv_b, mods[4], grad_nb)
    grad_ba = (grad_middle * mods[2]).astype(BF)
    go = rows_against(grad_ba, attended, out_tile * n_z, "grad_out")
    grad_att, = rows_times(
        places, grad_ba, w_mix, out_tile * n_z, 2 * out_tile, lambda v: (v.astype(BF),), (), (BF,), "grad_att"
    )
    block_out = from_clip(unplaced(middle + mods[5] * branch_b))
    grad_att, grad_middle, go, block_out = slot([gd], grad_att, grad_middle, go, block_out)
    go = sum_dp("out", go)
    out_rows = exchange("tokens_out", block_out, -1)
    grad_qkv, diag = attend_back(count, qkv, probs, grad_att, n_z)
    grad_qkv, diag = slot([go, out_rows], grad_qkv, diag)
    gq = rows_against(normed_a, grad_qkv, qkv_tile, "grad_qkv")
    gq, grad_qkv, gu = slot([go, out_rows], gq, grad_qkv, gu)
    gq = sum_dp("qkv", gq)
    grad_na = rows_times_t(places, grad_qkv, w_in, qkv_tile, "grad_normed_a")
    up_rows = shifted([gu[:, r * hidden_tile : (r + 1) * hidden_tile] for r in range(n_z)], n_z, -1)
    table = fold_bias(diag, place)
    grad_na, up_rows, table = slot([gq, go], grad_na, up_rows, table)
    out_up = functools.reduce(lambda a, b: a + b, [p.astype(F32) for p in up_rows])
    grad_tokens = from_clip(unplaced(grad_middle + norm_back(norm_a, inv_a, mods[1], grad_na)))
    in_rows = exchange("tokens_out", grad_tokens, -1)
    heads = table.shape[0] // n_z
    own = shifted([table[r * heads : (r + 1) * heads] for r in range(n_z)], n_z, -1)
    grad_mod = unplaced(
        jnp.stack(
            [
                jnp.sum(grad_na, axis=0),
                jnp.sum(grad_na * norm_a, axis=0),
                jnp.sum(grad_middle * branch_a, axis=0),
                jnp.sum(grad_nb, axis=0),
                jnp.sum(grad_nb * norm_b, axis=0),
                jnp.sum(grad_result * branch_b, axis=0),
            ]
        )
    ).reshape(1, n_z, -1)
    grad_mod = jnp.broadcast_to(grad_mod, (n_dp,) + grad_mod.shape[1:]).reshape(n_dp * n_z, -1)
    grad_mod, own = slot([gq, in_rows], grad_mod, functools.reduce(lambda a, b: a + b, own))

    table = butterfly("table", own, "dp", n_dp)
    block_out = by_clip(whole(out_rows))
    mod_cols = lax.all_to_all(grad_mod, ("dp", "tensor"), 0, 0, tiled=True)
    mod_cols, block_out, out_up = slot([gq, in_rows, table], mod_cols, block_out, out_up)
    pairs = [jnp.concatenate(p, axis=1) for p in zip(whole(gq), whole(go))]
    act_part = dot_nt(mod_cols, w_ada).reshape(n_dp, clips, feature)
    act_part = lax.all_to_all(act_part, "dp", 0, 0, tiled=True)
    act_part, pairs = slot([table], act_part, shifted(pairs, n_z, -1))
    pairs = functools.reduce(lambda a, b: a + b, [p.astype(F32) for p in pairs])
    grad_ada = dot_tn(cond_mine, mod_cols)
    grad_tokens = by_clip(whole(in_rows))
    act = butterfly("act", act_part, "tensor", n_z)
    slot([table, act])
    grad_act = whole(act).transpose(1, 0, 2).reshape(clips, model)
    grad_cond = jax.vjp(jax.nn.silu, cond_float)[1](grad_act)[0].reshape(conditioning.shape)
    grad_table = whole(table)
    return (
        block_out,
        grad_tokens,
        grad_cond,
        pairs[:, :qkv_tile].reshape(w_qkv.shape),
        pairs[:, qkv_tile:],
        out_up,
        whole(gd),
        grad_ada,
        grad_table,
    )


def solution(mesh):
    rows = P(None, "dp", None, "tensor", None)
    weight = P("dp", "tensor")
    qkv_weight = P("dp", None, "tensor")
    cond = P(None, "dp", None)
    table = P("tensor", None)
    return jax.shard_map(
        functools.partial(body, mesh.shape["dp"], mesh.shape["tensor"]),
        mesh=mesh,
        in_specs=(rows, cond, P(None, "dp"), qkv_weight, weight, weight, weight, weight, table, rows),
        out_specs=(rows, rows, cond, qkv_weight, weight, weight, weight, weight, table),
        check_vma=False,
    )
```

```python
import functools

import jax
import jax.numpy as jnp
import numpy as np
from jax import lax
from jax.experimental import pallas as pl
from jax.experimental.layout import Layout, with_layout_constraint
from jax.experimental.pallas import tpu as pltpu
from jax.sharding import PartitionSpec as P

HEAD_DIM = 64
WIN_T = 5
WIN_S = 8
FRAMES = 10
SPATIAL = 64
OFFSETS = 2025

EPSILON = 1e-06
NEGATIVE = -1e30
HIGHEST = lax.Precision.HIGHEST
BF = jnp.bfloat16
F32 = jnp.float32
WINDOWS = FRAMES // WIN_T
WIN_LEN = WIN_T * SPATIAL
SPREAD = 2 * WIN_T - 1
DIAG = SPREAD * SPATIAL
GROUPS = 4
VMEM = 48 << 20


def stage_bits(n_dp, core):
    bits = list(range(1, n_dp.bit_length() - 1))
    return bits if core == 0 else bits[::-1]


def stage_perm(n_dp, stage):
    return [(i, i ^ (1 << stage_bits(n_dp, i & 1)[stage])) for i in range(n_dp)]


def core_perm(n_dp):
    return [(i, i ^ 1) for i in range(n_dp)]


def ring(count, step):
    return [(i, (i + step) % count) for i in range(count)]


def stages(n_dp):
    return n_dp.bit_length() - 2


def dp_order(n_dp):
    half = n_dp // 2

    def mask(core, place):
        return sum(1 << b for t, b in enumerate(stage_bits(n_dp, core)) if place >> t & 1)

    return np.array(
        [[mask(c, k) for k in range(half)] + [1 ^ mask(1 - c, k) for k in range(half)] for c in (0, 1)],
        np.int32,
    )


def join(blocks, axis):
    return join_parts(blocks, axis, [blocks[0].shape[1]])[0]


def join_parts(blocks, axis, widths):
    rows, count = blocks[0].shape[0], len(blocks)

    def kernel(*refs):
        low = 0
        for out, width in zip(refs[count:], widths):
            for i, ref in enumerate(refs[:count]):
                if axis == 0:
                    out[i * rows : (i + 1) * rows, :] = ref[:, low : low + width]
                else:
                    out[:, i * width : (i + 1) * width] = ref[:, low : low + width]
            low += width

    shapes = [(rows * count, w) if axis == 0 else (rows, w * count) for w in widths]
    return pl.pallas_call(
        kernel,
        out_shape=[jax.ShapeDtypeStruct(s, blocks[0].dtype) for s in shapes],
        compiler_params=params(),
        cost_estimate=COST,
        name="join",
    )(*blocks)


def place_perm(n_dp, place):
    order = dp_order(n_dp)
    return [(i, i ^ int(order[i & 1, place])) for i in range(n_dp)]


def gather_steps(n_dp, n_z, rows, at_once):
    if at_once:
        rows = yield [rows] + [lax.ppermute(rows, "dp", place_perm(n_dp, k)) for k in range(1, n_dp // 2)]
    else:
        for t in range(stages(n_dp)):
            got = lax.ppermute(rows, "dp", stage_perm(n_dp, t))
            rows, got = yield rows, got
            rows = join([rows, got], 0) if t < stages(n_dp) - 1 else [rows, got]
    yield rows + [lax.ppermute(p, "dp", core_perm(n_dp)) for p in rows]


def add_low(first, *others):
    return functools.reduce(lambda a, b: a + b, [o.astype(F32) for o in others], first.astype(F32)).astype(BF)


def scatter_steps(n_dp, n_z, halves, at_once):
    keep, send = halves
    got = lax.ppermute(send, "dp", core_perm(n_dp))
    if at_once:
        count = n_dp // 2
        rows = keep.shape[0] // count
        mine = yield [add_low(keep[k * rows : (k + 1) * rows], got[k * rows : (k + 1) * rows]) for k in range(count)]
        terms = mine[:1] + [lax.ppermute(mine[k], "dp", place_perm(n_dp, k)) for k in range(1, count)]
    else:
        for t in range(stages(n_dp) - 1, -1, -1):
            rows = keep.shape[0] // 2
            keep, send = yield add_low(keep[:rows], got[:rows]), add_low(keep[rows:], got[rows:])
            got = lax.ppermute(send, "dp", stage_perm(n_dp, t))
        terms = [keep, got]
    if at_once:
        yield terms
        return
    width = terms[0].shape[1] // n_z
    yield [add_low(*(v[:, r * width : (r + 1) * width] for v in terms)) for r in range(n_z)]


def attention_parts(terms, beside, n_z):
    rows = beside.shape[0]
    wide, narrow = terms[0].shape[1] // n_z, beside.shape[1] // n_z

    def kernel(*refs):
        for r, out in enumerate(refs[-n_z:]):
            total = refs[0][:, r * wide : (r + 1) * wide].astype(F32)
            for ref in refs[1 : -n_z - 1]:
                total = total + ref[:, r * wide : (r + 1) * wide].astype(F32)
            out[:, :wide] = total.astype(BF)
            out[:, wide:] = refs[-n_z - 1][:, r * narrow : (r + 1) * narrow]

    return pl.pallas_call(
        kernel,
        out_shape=[jax.ShapeDtypeStruct((rows, wide + narrow), BF)] * n_z,
        compiler_params=params(),
        cost_estimate=COST,
        name="attention_parts",
    )(*terms, beside)


class Chain:
    def __init__(self, name, steps, total):
        self.name, self.steps, self.left, self.value = name, steps, total, None

    def step(self):
        with jax.named_scope(f"{self.name}_{self.left}_left"):
            self.value = self.steps.send(self.value)
        self.left -= 1


def slot(chains, *values, free=()):
    chains = [c for c in chains if c.left]
    for chain in chains + [c for c in free if c.left]:
        chain.step()
    held, values = lax.optimization_barrier(([c.value for c in chains], values))
    for chain, value in zip(chains, held):
        chain.value = value
    return values[0] if len(values) == 1 else values


def whole(chain):
    while chain.left:
        slot([chain])
    return chain.value


def shifted(pieces, n_z, sign):
    return [pieces[0]] + [lax.ppermute(pieces[r], "tensor", ring(n_z, sign * r)) for r in range(1, n_z)]


def exchange_steps(pieces, n_z, sign, first):
    pieces = list(pieces)
    for group in (first, [r for r in range(1, n_z) if r not in first]):
        for r in group:
            pieces[r] = lax.ppermute(pieces[r], "tensor", ring(n_z, sign * r))
        pieces = yield pieces


def butterfly_steps(value, axis, count):
    bit = 1
    while bit < count:
        value = yield value + lax.ppermute(value, axis, [(i, i ^ bit) for i in range(count)])
        bit *= 2


def pair_onehot(place):
    span = 2 * WIN_S - 1
    row, col = place // WIN_S, place % WIN_S
    offset = (row[None, :] - row[:, None] + WIN_S - 1) * span + (col[None, :] - col[:, None] + WIN_S - 1)
    return (jnp.arange(span * span)[:, None] == offset.reshape(1, -1)).astype(F32)


def spread_bias(table, place):
    heads = table.shape[0]
    flat = jnp.dot(table.reshape(heads * SPREAD, -1), pair_onehot(place), precision=HIGHEST)
    return flat.reshape(heads, SPREAD, SPATIAL, SPATIAL)


def fold_bias(diag, place):
    heads = diag.shape[0]
    rows = diag.reshape(heads * SPREAD, SPATIAL * SPATIAL)
    folded = lax.dot_general(rows, pair_onehot(place), (((1,), (1,)), ((), ())), precision=HIGHEST)
    return folded.reshape(heads, OFFSETS)


def dot(a, b):
    return jnp.dot(a, b, preferred_element_type=F32)


def dot_nt(a, b):
    return lax.dot_general(a, b, (((1,), (1,)), ((), ())), preferred_element_type=F32)


def dot_tn(a, b):
    return lax.dot_general(a, b, (((0,), (0,)), ((), ())), preferred_element_type=F32)


def params():
    return pltpu.CompilerParams(vmem_limit_bytes=VMEM)


COST = pl.CostEstimate(flops=10**6, bytes_accessed=10**4, transcendentals=0)


class Pieces:
    def __init__(self, arrays, width):
        self.arrays, self.width = arrays, width
        self.rows = sum(a.shape[0] for a in arrays)

    def specs(self):
        return [pl.BlockSpec((a.shape[0], self.width), lambda j, p: (0, j)) for a in self.arrays]

    def load(self, refs, places):
        return jnp.concatenate([r[...] for r in refs], axis=0)


class Gathered:
    def __init__(self, array, which, of):
        self.arrays, self.which, self.count = [array], which, array.shape[0]
        self.each = array.shape[2] // of
        self.rows = self.count * self.each

    def specs(self):
        n_dp, _, _, columns = self.arrays[0].shape
        return [pl.BlockSpec((n_dp, 1, self.each, columns), lambda j, p: (0, p[n_dp + j], self.which, 0))]

    def load(self, refs, places):
        return jnp.concatenate([refs[0][places[k], 0] for k in range(self.count)], axis=0)


def rows_times(places, x, weight, columns, tile, finish, extra, outs, name):
    length, depth = x.shape
    count = len(weight.arrays)

    def kernel(places_ref, x_ref, *refs):
        w = weight.load(refs[:count], places_ref)
        done = finish(dot(x_ref[...], w), *(r[...] for r in refs[count : count + len(extra)]))
        for ref, value in zip(refs[count + len(extra) :], done):
            ref[...] = value

    tall = pl.BlockSpec((length, tile), lambda j, p: (0, j))
    return pl.pallas_call(
        kernel,
        grid_spec=pltpu.PrefetchScalarGridSpec(
            num_scalar_prefetch=1,
            grid=(columns // tile,),
            in_specs=[pl.BlockSpec((length, depth), lambda j, p: (0, 0))] + weight.specs() + [tall] * len(extra),
            out_specs=[tall] * len(outs),
        ),
        out_shape=[jax.ShapeDtypeStruct((length, columns), t) for t in outs],
        compiler_params=params(),
        cost_estimate=COST,
        name=name,
    )(places, x, *weight.arrays, *extra)


def rows_times_t(places, x, weight, tile, finish, by_row, const, row_outs, sums, name):
    length, depth = x.shape
    count, steps, chunk = len(weight.arrays), depth // tile, SPATIAL * 2
    n_by, n_const, n_out = len(by_row), len(const), len(row_outs)

    def kernel(places_ref, x_ref, *refs):
        parts = iter(refs)
        w_refs, by_refs, const_refs, out_refs = ([next(parts) for _ in range(n)] for n in (count, n_by, n_const, n_out))
        sum_ref = next(parts) if sums else None
        acc = next(parts)
        term = dot_nt(x_ref[...], weight.load(w_refs, places_ref))

        @pl.when(pl.program_id(0) == 0)
        def _():
            acc[...] = term

        @pl.when(pl.program_id(0) > 0)
        def _():
            acc[...] += term

        @pl.when(pl.program_id(0) == steps - 1)
        def _():
            totals = None
            for i in range(0, length, chunk):
                rows = slice(i, i + chunk)
                done, adds = finish(acc[rows], *(r[rows] for r in by_refs), *(r[...] for r in const_refs))
                for ref, value in zip(out_refs, done):
                    ref[rows] = value
                adds = [jnp.sum(v, axis=0, keepdims=True) for v in adds]
                totals = adds if totals is None else [t + v for t, v in zip(totals, adds)]
            if sums:
                sum_ref[...] = jnp.concatenate(totals, axis=0)

    def full(shape):
        return pl.BlockSpec(shape, lambda j, p: (0, 0))

    shapes = [jax.ShapeDtypeStruct(s, t) for s, t in row_outs]
    if sums:
        shapes.append(jax.ShapeDtypeStruct((sums, weight.rows), F32))
    return pl.pallas_call(
        kernel,
        grid_spec=pltpu.PrefetchScalarGridSpec(
            num_scalar_prefetch=1,
            grid=(steps,),
            in_specs=[pl.BlockSpec((length, tile), lambda j, p: (0, j))]
            + weight.specs()
            + [full(v.shape) for v in (*by_row, *const)],
            out_specs=[full(v.shape) for v in shapes],
            scratch_shapes=[pltpu.VMEM((length, weight.rows), F32)],
        ),
        out_shape=shapes,
        compiler_params=params(),
        cost_estimate=COST,
        name=name,
    )(places, x, *weight.arrays, *by_row, *const)


def rows_against(x, y, tile, name, places=None, n_dp=1):
    length, depth = x.shape
    columns = y.shape[1]
    rows = depth // n_dp

    def kernel(places_ref, x_ref, y_ref, *refs):
        turned = refs[-1]

        @pl.when(pl.program_id(0) == 0)
        def _():
            turned[...] = x_ref[...].T

        result = dot(turned[...], y_ref[...]).astype(BF)
        if n_dp == 1:
            refs[0][...] = result[: depth // 2]
            refs[1][...] = result[depth // 2 :]
        else:
            for k in range(n_dp):
                refs[0][places_ref[k]] = result[k * rows : (k + 1) * rows]

    if n_dp == 1:
        shape = jax.ShapeDtypeStruct((depth // 2, columns), BF)
        half = pl.BlockSpec((depth // 2, tile), lambda j, p: (0, j))
        out_shape, out_specs = [shape, shape], [half, half]
        places = jnp.zeros((1,), jnp.int32)
    else:
        out_shape = jax.ShapeDtypeStruct((n_dp, rows, columns), BF)
        out_specs = pl.BlockSpec((n_dp, rows, tile), lambda j, p: (0, 0, j))
    return pl.pallas_call(
        kernel,
        grid_spec=pltpu.PrefetchScalarGridSpec(
            num_scalar_prefetch=1,
            grid=(columns // tile,),
            in_specs=[
                pl.BlockSpec((length, depth), lambda j, p: (0, 0)),
                pl.BlockSpec((length, tile), lambda j, p: (0, j)),
            ],
            out_specs=out_specs,
            scratch_shapes=[pltpu.VMEM((depth, length), BF)],
        ),
        out_shape=out_shape,
        compiler_params=params(),
        cost_estimate=COST,
        name=name,
    )(places, x, y)


def head_cols(kind, h, width):
    return slice(kind * width + h * HEAD_DIM, kind * width + (h + 1) * HEAD_DIM)


def attend_kernel(heads, count_ref, qkv_ref, bias_ref, att_ref, prob_ref):
    width = heads * HEAD_DIM
    scale = jnp.asarray(HEAD_DIM**-0.5, BF)
    key_at = lax.broadcasted_iota(jnp.int32, (WIN_LEN, WIN_LEN), 0)
    row_at = lax.broadcasted_iota(jnp.int32, (WIN_LEN, width), 0)
    att = [[] for _ in range(WINDOWS)]
    for h in range(heads):
        bias = jnp.concatenate(
            [
                jnp.concatenate([bias_ref[h, a - b + WIN_T - 1] for a in range(WIN_T)], axis=1)
                for b in range(WIN_T)
            ],
            axis=0,
        )
        for w in range(WINDOWS):
            live = (count_ref[0] - w * WIN_T) * SPATIAL
            rows = slice(w * WIN_LEN, (w + 1) * WIN_LEN)
            q = qkv_ref[rows, head_cols(0, h, width)] * scale
            k = qkv_ref[rows, head_cols(1, h, width)]
            v = qkv_ref[rows, head_cols(2, h, width)]
            scores = jnp.where(key_at < live, dot_nt(k, q) + bias, NEGATIVE)
            top = jnp.max(scores, axis=0, keepdims=True)
            expo = jnp.exp(scores - top)
            total = jnp.maximum(jnp.sum(expo, axis=0, keepdims=True), 1.0)
            probs = (expo * jnp.where(live > 0, 1.0 / total, 0.0)).astype(BF)
            prob_ref[w, h] = probs
            att[w].append(dot_tn(v, probs))
    for w in range(WINDOWS):
        live = (count_ref[0] - w * WIN_T) * SPATIAL
        whole = jnp.concatenate(att[w], axis=0).T
        att_ref[w * WIN_LEN : (w + 1) * WIN_LEN, :] = jnp.where(row_at < live, whole, 0.0).astype(BF)


def attend_back_kernel(heads, count_ref, qkv_ref, prob_ref, gatt_ref, gqkv_ref, diag_ref):
    width = heads * HEAD_DIM
    scale = jnp.asarray(HEAD_DIM**-0.5, BF)
    row_at = lax.broadcasted_iota(jnp.int32, (WIN_LEN, HEAD_DIM), 0)
    grad_q = [[] for _ in range(WINDOWS)]
    for h in range(heads):
        both = None
        for w in range(WINDOWS):
            live = (count_ref[0] - w * WIN_T) * SPATIAL
            rows = slice(w * WIN_LEN, (w + 1) * WIN_LEN)
            q = qkv_ref[rows, head_cols(0, h, width)] * scale
            k = qkv_ref[rows, head_cols(1, h, width)] * scale
            v = qkv_ref[rows, head_cols(2, h, width)]
            gatt = gatt_ref[rows, head_cols(0, h, width)]
            gatt = jnp.where(row_at < live, gatt, jnp.zeros_like(gatt))
            probs = prob_ref[w, h]
            full = probs.astype(F32)
            gqkv_ref[rows, head_cols(2, h, width)] = dot(probs, gatt).astype(BF)
            gprobs = dot_nt(v, gatt)
            inner = jnp.sum(full * gprobs, axis=0, keepdims=True)
            gscores = (full * (gprobs - inner)).astype(BF)
            gqkv_ref[rows, head_cols(1, h, width)] = dot(gscores, q).astype(BF)
            grad_q[w].append(dot_tn(k, gscores))
            wide = gscores.astype(F32)
            both = wide if both is None else both + wide
        blocks = [both[b * SPATIAL : (b + 1) * SPATIAL] for b in range(WIN_T)]
        for t in range(SPREAD):
            pairs = [(b, b + t - WIN_T + 1) for b in range(WIN_T) if 0 <= b + t - WIN_T + 1 < WIN_T]
            diag_ref[h, t] = functools.reduce(
                lambda x, y: x + y, [blocks[b][:, a * SPATIAL : (a + 1) * SPATIAL] for b, a in pairs]
            )
    for w in range(WINDOWS):
        whole = jnp.concatenate(grad_q[w], axis=0).T
        gqkv_ref[w * WIN_LEN : (w + 1) * WIN_LEN, 0:width] = whole.astype(BF)


def attend(count, qkv, bias, n_z):
    heads = bias.shape[0] // n_z
    width = heads * HEAD_DIM
    length = WINDOWS * WIN_LEN
    return pl.pallas_call(
        functools.partial(attend_kernel, heads),
        grid_spec=pltpu.PrefetchScalarGridSpec(
            num_scalar_prefetch=1,
            grid=(n_z,),
            in_specs=[
                pl.BlockSpec((length, 3 * width), lambda r, c: (0, r)),
                pl.BlockSpec((heads, SPREAD, SPATIAL, SPATIAL), lambda r, c: (r, 0, 0, 0)),
            ],
            out_specs=[
                pl.BlockSpec((length, width), lambda r, c: (0, r)),
                pl.BlockSpec((WINDOWS, heads, WIN_LEN, WIN_LEN), lambda r, c: (0, r, 0, 0)),
            ],
        ),
        out_shape=[
            jax.ShapeDtypeStruct((length, n_z * width), BF),
            jax.ShapeDtypeStruct((WINDOWS, n_z * heads, WIN_LEN, WIN_LEN), BF),
        ],
        compiler_params=params(),
        cost_estimate=COST,
        name="attend",
    )(count, qkv, bias)


def attend_back(count, qkv, probs, gatt, n_z):
    heads = probs.shape[1] // n_z
    width = heads * HEAD_DIM
    length = WINDOWS * WIN_LEN
    return pl.pallas_call(
        functools.partial(attend_back_kernel, heads),
        grid_spec=pltpu.PrefetchScalarGridSpec(
            num_scalar_prefetch=1,
            grid=(n_z,),
            in_specs=[
                pl.BlockSpec((length, 3 * width), lambda r, c: (0, r)),
                pl.BlockSpec((WINDOWS, heads, WIN_LEN, WIN_LEN), lambda r, c: (0, r, 0, 0)),
                pl.BlockSpec((length, width), lambda r, c: (0, r)),
            ],
            out_specs=[
                pl.BlockSpec((length, 3 * width), lambda r, c: (0, r)),
                pl.BlockSpec((heads, SPREAD, SPATIAL, SPATIAL), lambda r, c: (r, 0, 0, 0)),
            ],
        ),
        out_shape=[
            jax.ShapeDtypeStruct((length, n_z * 3 * width), BF),
            jax.ShapeDtypeStruct((n_z * heads, SPREAD, SPATIAL, SPATIAL), F32),
        ],
        compiler_params=params(),
        cost_estimate=COST,
        name="attend_back",
    )(count, qkv, probs, gatt)


def normalize(values):
    center = values - jnp.mean(values, axis=-1, keepdims=True)
    scale = lax.rsqrt(jnp.mean(center * center, axis=-1, keepdims=True) + EPSILON)
    return center * scale, scale


def norm_back(normed, inv_sigma, scale_row, grad):
    u = (1.0 + scale_row) * grad
    return (u - jnp.mean(u, axis=-1, keepdims=True) - normed * jnp.mean(u * normed, axis=-1, keepdims=True)) * inv_sigma


def after_attention(branch_a, resid, mods):
    middle = resid.astype(F32) + mods[2:3] * branch_a
    normed = (normalize(middle)[0] * (1.0 + mods[4:5]) + mods[3:4]).astype(BF)
    return (branch_a, middle, normed), ()


def after_mlp(branch_b, middle, grad_result, mods, to_place):
    result = (middle + mods[5:6] * branch_b).astype(BF)
    return (dot_nt(result, to_place).astype(BF),), (grad_result.astype(F32) * branch_b,)


def back_mlp(grad_nb, middle, branch_a, grad_result, mods):
    norm_b, inv_b = normalize(middle)
    grad_middle = grad_result.astype(F32) + norm_back(norm_b, inv_b, mods[4:5], grad_nb)
    return (
        (grad_middle, (grad_middle * mods[2:3]).astype(BF)),
        (grad_middle * branch_a, grad_nb, grad_nb * norm_b),
    )


def back_attention(grad_na, resid, grad_middle, mods, to_place):
    norm_a, inv_a = normalize(resid.astype(F32))
    grad_tokens = (grad_middle + norm_back(norm_a, inv_a, mods[1:2], grad_na)).astype(BF)
    return (dot_nt(grad_tokens, to_place).astype(BF),), (grad_na, grad_na * norm_a)


def gelu_and_slope(v):
    c = float(np.sqrt(2 / np.pi))
    square = v * v
    h = 0.5 + 0.5 * jnp.tanh(v * (c + (0.044715 * c) * square))
    slope = h + h * (1.0 - h) * (v * (2 * c + (6 * 0.044715 * c) * square))
    return (v * h).astype(BF), slope.astype(BF)


def body(
    n_dp, n_z, tokens, conditioning, frame_counts, w_qkv, w_out, w_up, w_down, w_ada, pos_table, cotangent
):
    micro, clip_dev, _, part, model = tokens.shape
    clips = micro * clip_dev
    assert clips == n_z and part * n_z == SPATIAL
    feature = model // n_dp
    qkv_tile, hidden_tile, out_tile = 3 * w_out.shape[1], w_up.shape[1], w_out.shape[1]
    d, z = lax.axis_index("dp"), lax.axis_index("tensor")
    count = lax.dynamic_slice_in_dim(frame_counts.reshape(clips), z, 1)

    order = jnp.asarray(dp_order(n_dp))[d & 1] ^ d
    source = (order[:, None] * feature + jnp.arange(feature)[None, :]).reshape(1, model)
    to_place = (jnp.arange(model)[:, None] == source).astype(BF)

    places = jnp.concatenate([order, (z - jnp.arange(n_z)) % n_z]).astype(jnp.int32)

    def placed(rows):
        return dot(rows, to_place).astype(BF)

    def unplaced(rows):
        return dot_nt(rows.astype(BF), to_place).astype(BF)

    place = jnp.arange(SPATIAL)
    place = (z - place // part) % n_z * part + place % part

    def for_clips(rows):
        rows = rows.reshape(clips, FRAMES, part, model)
        return [lax.dynamic_index_in_dim(rows, (z + r) % n_z, 0, False) for r in range(n_z)]

    def to_clip(parts):
        with jax.named_scope("tokens_in"):
            return shifted(parts, n_z, 1)

    def in_order(got):
        return placed(jnp.stack(got, axis=1).reshape(FRAMES * SPATIAL, model))

    def from_clip(rows):
        rows = rows.reshape(FRAMES, n_z, part, model)
        return [rows[:, r] for r in range(n_z)]

    def by_clip(got):
        whole_rows = jnp.zeros((clips, FRAMES, part, model), BF)
        for r in range(n_z):
            whole_rows = lax.dynamic_update_index_in_dim(whole_rows, got[r], (z + r) % n_z, 0)
        return whole_rows.reshape(tokens.shape)

    few = stages(n_dp) == 2

    def gather(name, shard, at_once=False):
        at_once = at_once and few
        return Chain("gather_" + name, gather_steps(n_dp, n_z, shard, at_once), 1 + (1 if at_once else stages(n_dp)))

    def sum_dp(name, halves, at_once=False):
        return Chain("scatter_" + name, scatter_steps(n_dp, n_z, halves, at_once), 1 + (1 if at_once else stages(n_dp)))

    def exchange(name, pieces, sign, first=(n_z // 2,)):
        return Chain(name, exchange_steps(pieces, n_z, sign, first), 2)

    def butterfly(name, value, axis, size):
        return Chain(name, butterfly_steps(value, axis, size), size.bit_length() - 1)

    mlp = lax.all_gather(jnp.concatenate([w_up, w_down], axis=0), ("dp", "tensor"), axis=0)
    wu, wd = (Gathered(mlp.reshape(n_dp, n_z, -1, w_up.shape[1]), i, 2) for i in (0, 1))

    def turned(blocks):
        return jnp.concatenate([lax.dynamic_slice_in_dim(blocks, (z - r) % n_z, 1) for r in range(n_z)], axis=0)

    cond_float = conditioning.astype(F32).reshape(clips, model)
    cond_act = jax.nn.silu(cond_float).astype(BF)
    cond_mine = lax.all_to_all(
        cond_act.reshape(clips, n_dp, feature).transpose(1, 0, 2), "dp", 0, 0, tiled=True
    ).reshape(n_dp * clips, feature)
    share = -(-pos_table.size // n_dp)
    table = jnp.pad(pos_table.reshape(-1), (0, share * n_dp - pos_table.size)).reshape(n_dp, share)
    table = jnp.broadcast_to(lax.dynamic_slice_in_dim(table, d, 1), (n_dp * n_z, share))
    mod_part = dot(cond_mine, w_ada)
    columns = mod_part.shape[1]
    mod_part = lax.all_to_all(jnp.concatenate([mod_part, table], axis=1), ("dp", "tensor"), 0, 0, tiled=True)
    blocks = shifted([jnp.concatenate([w_qkv.reshape(feature, -1), w_out], axis=1)] * n_z, n_z, 1)
    blocks, to_place, got_tokens, places, count, mod_part = slot(
        [], blocks, to_place, for_clips(tokens), places, count, mod_part
    )
    wa, wo = join_parts(blocks, 1, [qkv_tile, out_tile])
    wa, wo = gather("qkv", wa, True), gather("out", wo, True)
    table = mod_part[:, columns:].reshape(n_dp, n_z, share).transpose(1, 0, 2).reshape(n_z, -1)[:, : pos_table.size]
    mods = jnp.sum(mod_part[:, :columns].reshape(n_dp, n_z, -1), axis=0).reshape(6, model)
    mods = jnp.dot(mods, to_place.astype(F32), precision=HIGHEST)
    bias = with_layout_constraint(spread_bias(turned(table).reshape(-1, OFFSETS), place), Layout((0, 1, 2, 3)))
    got_tokens, bias, mods = slot([wa], to_clip(got_tokens), bias, mods)
    resid = in_order(got_tokens)
    normed_a = (normalize(resid.astype(F32))[0] * (1.0 + mods[1:2]) + mods[0:1]).astype(BF)
    normed_a = slot([wa], normed_a)
    rows_of = (FRAMES * SPATIAL, model)

    w_in = Pieces(whole(wa), qkv_tile)
    qkv, = rows_times(places, normed_a, w_in, qkv_tile * n_z, qkv_tile, lambda v: (v.astype(BF),), (), (BF,), "qkv")
    qkv = slot([wo], qkv)
    attended, probs = attend(count, qkv, bias, n_z)
    attended, probs, got_cotangent = slot([wo], attended, probs, for_clips(cotangent))
    got_cotangent = to_clip(got_cotangent)
    wo = Pieces(whole(wo), out_tile * n_z)
    branch_a, middle, normed_b = rows_times_t(
        places, attended, wo, out_tile * n_z, after_attention, (resid,), (mods,),
        ((rows_of, F32), (rows_of, F32), (rows_of, BF)), 0, "out",
    )
    activ, slope = rows_times(places, normed_b, wu, hidden_tile * n_z, hidden_tile, gelu_and_slope, (), (BF, BF), "up")
    activ, slope, got_cotangent = slot([], activ, slope, got_cotangent)
    grad_result = in_order(got_cotangent)
    grad_bb = (grad_result.astype(F32) * mods[5:6]).astype(BF)
    gd = rows_against(grad_bb, activ, hidden_tile, "grad_down")
    activ, slope, grad_bb, gd = slot([], activ, slope, grad_bb, gd)
    gd = sum_dp("down", gd)

    grad_hidden, = rows_times(
        places, grad_bb, wd, hidden_tile * n_z, hidden_tile, lambda v, s: ((v * s.astype(F32)).astype(BF),), (slope,), (BF,),
        "grad_hidden",
    )
    grad_hidden, activ = slot([gd], grad_hidden, activ)
    gu = rows_against(normed_b, grad_hidden, hidden_tile, "grad_up")
    block_out, sums_mlp = rows_times_t(
        places, activ, wd, hidden_tile, after_mlp, (middle, grad_result), (mods, to_place), ((rows_of, BF),), 1, "down"
    )
    grad_hidden, gu, block_out = slot([gd], grad_hidden, gu, from_clip(block_out))
    gu = sum_dp("up", gu)
    out_rows = exchange("tokens_out", block_out, -1)
    grad_middle, grad_ba, sums_mid = rows_times_t(
        places, grad_hidden, wu, hidden_tile, back_mlp, (middle, branch_a, grad_result), (mods,),
        ((rows_of, F32), (rows_of, BF)), 3, "grad_normed_b",
    )
    grad_middle, grad_ba = slot([gd, gu, out_rows], grad_middle, grad_ba)
    down_rows = exchange("down_sum", whole(gd), -1)
    go = rows_against(grad_ba, attended, out_tile * n_z, "grad_out", places, n_dp)
    grad_att, = rows_times(
        places, grad_ba, wo, out_tile * n_z, out_tile * n_z, lambda v: (v.astype(BF),), (), (BF,), "grad_att"
    )
    grad_qkv, diag = attend_back(count, qkv, probs, grad_att, n_z)
    grad_qkv, diag, go = slot([gu, down_rows, out_rows], grad_qkv, diag, go)
    go = lax.psum_scatter(go.reshape(model, -1), "dp", scatter_dimension=0, tiled=True)
    gq = rows_against(normed_a, grad_qkv, qkv_tile, "grad_qkv")
    table = turned(fold_bias(diag, place).reshape(n_z, -1, OFFSETS))
    table = jnp.pad(table, ((0, 0), (0, 0), (0, -OFFSETS % n_dp)))
    table = table.reshape(n_z, -1, n_dp, table.shape[2] // n_dp).transpose(2, 0, 1, 3)
    table = table.reshape((n_dp * n_z,) + table.shape[2:])
    gq, grad_qkv, table = slot([gu, down_rows], gq, grad_qkv, table)
    gq = sum_dp("qkv", gq, few)
    up_rows = exchange("up_sum", whole(gu), -1)
    grad_tokens, sums_in = rows_times_t(
        places, grad_qkv, w_in, qkv_tile, back_attention, (resid, grad_middle), (mods, to_place), ((rows_of, BF),), 2,
        "grad_normed_a",
    )
    up_rows.step()
    in_rows = exchange("tokens_out", from_clip(grad_tokens), -1)
    in_rows.step()
    sums_in, block_out = slot([gq, up_rows], sums_in, whole(out_rows))
    in_rows.step()
    gq.step()
    if few:
        gq.value[1], sums_in = lax.optimization_barrier((gq.value[1], sums_in))
    grad_mod = unplaced(jnp.concatenate([sums_in, sums_mid, sums_mlp], axis=0)).reshape(1, n_z, -1)
    grad_mod = jnp.broadcast_to(grad_mod, (n_dp,) + grad_mod.shape[1:]).reshape(n_dp * n_z, -1).astype(F32)
    small = jnp.concatenate([grad_mod, table.reshape(n_dp * n_z, -1)], axis=1)
    small = lax.all_to_all(small, ("dp", "tensor"), 0, 0, tiled=True)
    gq.value, small, grad_tokens, go = slot([], gq.value, small, in_rows.value, go)

    terms = whole(gq) if few else [jnp.concatenate(whole(gq), axis=1)]
    pairs = attention_parts(terms, go, n_z)
    pairs, small = lax.optimization_barrier((pairs, small))
    pairs = functools.reduce(lambda a, b: a + b, [p.astype(F32) for p in shifted(pairs, n_z, -1)])
    mod_cols = small[:, :columns].astype(BF)
    act_part = dot_nt(mod_cols, w_ada).reshape(n_dp, 1, -1)
    act_part = jnp.broadcast_to(act_part, (n_dp, n_z, act_part.shape[2])).reshape(n_dp * n_z, -1)
    table = jnp.sum(small[:, columns:], axis=0)
    table = jnp.broadcast_to(table[None], (n_dp * n_z, table.shape[0]))
    small = lax.all_to_all(jnp.concatenate([act_part, table], axis=1), ("dp", "tensor"), 0, 0, tiled=True)
    small = small.reshape(n_dp, n_z, -1)
    grad_act = jnp.sum(small[:, :, : clips * feature], axis=1).reshape(n_dp, clips, feature)
    grad_act = grad_act.transpose(1, 0, 2).reshape(clips, model)
    grad_cond = jax.vjp(jax.nn.silu, cond_float)[1](grad_act)[0].reshape(conditioning.shape)
    table = lax.dynamic_index_in_dim(small[:, :, clips * feature :], z, 1, False)
    table = table.reshape(n_dp, pos_table.shape[0], -1).transpose(1, 0, 2)
    grad_table = table.reshape(pos_table.shape[0], -1)[:, :OFFSETS]
    grad_ada = dot_tn(cond_mine, mod_cols)
    block_out, grad_tokens = by_clip(block_out), by_clip(grad_tokens)
    out_down, out_up = (
        functools.reduce(lambda a, b: a + b, [p.astype(F32) for p in whole(rows)]) for rows in (down_rows, up_rows)
    )
    return (
        block_out,
        grad_tokens,
        grad_cond,
        pairs[:, :qkv_tile].reshape(w_qkv.shape),
        pairs[:, qkv_tile:],
        out_up,
        out_down,
        grad_ada,
        grad_table,
    )


def solution(mesh):
    rows = P(None, "dp", None, "tensor", None)
    weight = P("dp", "tensor")
    qkv_weight = P("dp", None, "tensor")
    cond = P(None, "dp", None)
    table = P("tensor", None)
    return jax.shard_map(
        functools.partial(body, mesh.shape["dp"], mesh.shape["tensor"]),
        mesh=mesh,
        in_specs=(rows, cond, P(None, "dp"), qkv_weight, weight, weight, weight, weight, table, rows),
        out_specs=(rows, rows, cond, qkv_weight, weight, weight, weight, weight, table),
        check_vma=False,
    )
```

```python
import functools

import jax
import jax.numpy as jnp
import numpy as np
from jax import lax
from jax.experimental import pallas as pl
from jax.experimental.layout import Layout, with_layout_constraint
from jax.experimental.pallas import tpu as pltpu
from jax.sharding import PartitionSpec as P

HEAD_DIM = 64
WIN_T = 5
WIN_S = 8
FRAMES = 10
SPATIAL = 64
OFFSETS = 2025

EPSILON = 1e-06
NEGATIVE = -1e30
HIGHEST = lax.Precision.HIGHEST
BF = jnp.bfloat16
F32 = jnp.float32
WINDOWS = FRAMES // WIN_T
WIN_LEN = WIN_T * SPATIAL
SPREAD = 2 * WIN_T - 1
DIAG = SPREAD * SPATIAL
GROUPS = 4


def stage_bits(n_dp, core):
    bits = list(range(1, n_dp.bit_length() - 1))
    return bits if core == 0 else bits[::-1]


def stage_perm(n_dp, stage):
    return [(i, i ^ (1 << stage_bits(n_dp, i & 1)[stage])) for i in range(n_dp)]


def core_perm(n_dp):
    return [(i, i ^ 1) for i in range(n_dp)]


def ring(count, step):
    return [(i, (i + step) % count) for i in range(count)]


def stages(n_dp):
    return n_dp.bit_length() - 2


def dp_order(n_dp):
    half = n_dp // 2

    def mask(core, place):
        return sum(1 << b for t, b in enumerate(stage_bits(n_dp, core)) if place >> t & 1)

    return np.array(
        [[mask(c, k) for k in range(half)] + [1 ^ mask(1 - c, k) for k in range(half)] for c in (0, 1)],
        np.int32,
    )


def join(blocks, axis):
    return join_parts(blocks, axis, [blocks[0].shape[1]])[0]


def join_parts(blocks, axis, widths):
    rows, count = blocks[0].shape[0], len(blocks)

    def kernel(*refs):
        low = 0
        for out, width in zip(refs[count:], widths):
            for i, ref in enumerate(refs[:count]):
                if axis == 0:
                    out[i * rows : (i + 1) * rows, :] = ref[:, low : low + width]
                else:
                    out[:, i * width : (i + 1) * width] = ref[:, low : low + width]
            low += width

    shapes = [(rows * count, w) if axis == 0 else (rows, w * count) for w in widths]
    return pl.pallas_call(
        kernel,
        out_shape=[jax.ShapeDtypeStruct(s, blocks[0].dtype) for s in shapes],
        compiler_params=params(),
        cost_estimate=COST,
        name="join",
    )(*blocks)


def place_perm(n_dp, place):
    order = dp_order(n_dp)
    return [(i, i ^ int(order[i & 1, place])) for i in range(n_dp)]


def gather_steps(n_dp, n_z, rows, at_once):
    if at_once:
        rows = yield [rows] + [lax.ppermute(rows, "dp", place_perm(n_dp, k)) for k in range(1, n_dp // 2)]
    else:
        for t in range(stages(n_dp)):
            got = lax.ppermute(rows, "dp", stage_perm(n_dp, t))
            rows, got = yield rows, got
            rows = join([rows, got], 0) if t < stages(n_dp) - 1 else [rows, got]
    yield rows + [lax.ppermute(p, "dp", core_perm(n_dp)) for p in rows]


def add_low(first, *others):
    return functools.reduce(lambda a, b: a + b, [o.astype(F32) for o in others], first.astype(F32)).astype(BF)


def scatter_steps(n_dp, n_z, halves, at_once):
    keep, send = halves
    got = lax.ppermute(send, "dp", core_perm(n_dp))
    if at_once:
        count = n_dp // 2
        rows = keep.shape[0] // count
        mine = [add_low(keep[k * rows : (k + 1) * rows], got[k * rows : (k + 1) * rows]) for k in range(count)]
        sent = yield mine[1:]
        far = lax.ppermute(sent[-1], "dp", place_perm(n_dp, count - 1))
        terms = mine[:1] + [lax.ppermute(v, "dp", place_perm(n_dp, k + 1)) for k, v in enumerate(sent[:-1])] + [far]
    else:
        for t in range(stages(n_dp) - 1, -1, -1):
            rows = keep.shape[0] // 2
            send, = yield [add_low(keep[rows:], got[rows:])]
            keep = add_low(keep[:rows], got[:rows])
            got = lax.ppermute(send, "dp", stage_perm(n_dp, t))
        terms = [keep, got]
    if at_once:
        yield terms
        return
    width = terms[0].shape[1] // n_z
    yield [add_low(*(v[:, r * width : (r + 1) * width] for v in terms)) for r in range(n_z)]


def attention_parts(terms, beside, n_z):
    rows = beside.shape[0]
    wide, narrow = terms[0].shape[1] // n_z, beside.shape[1] // n_z

    def kernel(*refs):
        for r, out in enumerate(refs[-n_z:]):
            total = refs[0][:, r * wide : (r + 1) * wide].astype(F32)
            for ref in refs[1 : -n_z - 1]:
                total = total + ref[:, r * wide : (r + 1) * wide].astype(F32)
            out[:, :wide] = total.astype(BF)
            out[:, wide:] = refs[-n_z - 1][:, r * narrow : (r + 1) * narrow]

    return pl.pallas_call(
        kernel,
        out_shape=[jax.ShapeDtypeStruct((rows, wide + narrow), BF)] * n_z,
        compiler_params=params(),
        cost_estimate=COST,
        name="attention_parts",
    )(*terms, beside)


class Chain:
    def __init__(self, name, steps, total):
        self.name, self.steps, self.left, self.value = name, steps, total, None

    def step(self):
        with jax.named_scope(f"{self.name}_{self.left}_left"):
            self.value = self.steps.send(self.value)
        self.left -= 1


def slot(chains, *values, free=()):
    chains = [c for c in chains if c.left]
    for chain in chains + [c for c in free if c.left]:
        chain.step()
    held, values = lax.optimization_barrier(([c.value for c in chains], values))
    for chain, value in zip(chains, held):
        chain.value = value
    return values[0] if len(values) == 1 else values


def whole(chain):
    while chain.left:
        slot([chain])
    return chain.value


def shifted(pieces, n_z, sign):
    return [pieces[0]] + [lax.ppermute(pieces[r], "tensor", ring(n_z, sign * r)) for r in range(1, n_z)]


def exchange_steps(pieces, n_z, sign, first):
    pieces = list(pieces)
    for group in (first, [r for r in range(1, n_z) if r not in first]):
        for r in group:
            pieces[r] = lax.ppermute(pieces[r], "tensor", ring(n_z, sign * r))
        pieces = yield pieces


def butterfly_steps(value, axis, count):
    bit = 1
    while bit < count:
        value = yield value + lax.ppermute(value, axis, [(i, i ^ bit) for i in range(count)])
        bit *= 2


def pair_onehot(place):
    span = 2 * WIN_S - 1
    row, col = place // WIN_S, place % WIN_S
    offset = (row[None, :] - row[:, None] + WIN_S - 1) * span + (col[None, :] - col[:, None] + WIN_S - 1)
    return (jnp.arange(span * span)[:, None] == offset.reshape(1, -1)).astype(F32)


def spread_bias(table, place):
    heads = table.shape[0]
    flat = jnp.dot(table.reshape(heads * SPREAD, -1), pair_onehot(place), precision=HIGHEST)
    return flat.reshape(heads, SPREAD, SPATIAL, SPATIAL)


def fold_bias(diag, place):
    heads = diag.shape[0]
    rows = diag.reshape(heads * SPREAD, SPATIAL * SPATIAL)
    folded = lax.dot_general(rows, pair_onehot(place), (((1,), (1,)), ((), ())), precision=HIGHEST)
    return folded.reshape(heads, OFFSETS)


def dot(a, b):
    return jnp.dot(a, b, preferred_element_type=F32)


def dot_nt(a, b):
    return lax.dot_general(a, b, (((1,), (1,)), ((), ())), preferred_element_type=F32)


def dot_tn(a, b):
    return lax.dot_general(a, b, (((0,), (0,)), ((), ())), preferred_element_type=F32)


def params(mib=28):
    return pltpu.CompilerParams(vmem_limit_bytes=mib << 20)


COST = pl.CostEstimate(flops=10**6, bytes_accessed=10**4, transcendentals=0)


class Pieces:
    def __init__(self, arrays, width, n_dp):
        self.arrays, self.width, self.n_dp = arrays, width, n_dp
        self.rows = sum(a.shape[0] for a in arrays)

    def specs(self):
        return [pl.BlockSpec((a.shape[0], self.width), lambda j, p: (0, j)) for a in self.arrays]

    def load(self, refs, places):
        return jnp.concatenate([r[...] for r in refs], axis=0)


class Gathered:
    def __init__(self, array, rows):
        self.arrays, self.each, self.n_dp = [array], rows, array.shape[0]
        self.rows = self.n_dp * rows

    def specs(self):
        n_dp, _, _, columns = self.arrays[0].shape
        return [pl.BlockSpec((n_dp, 1, self.each, columns), lambda j, p: (0, p[n_dp + j], 0, 0))]

    def load(self, refs, places):
        return jnp.concatenate([refs[0][places[k], 0] for k in range(self.n_dp)], axis=0)


class Folded:
    def __init__(self, array, before, rows, width):
        self.arrays, self.before, self.width = [array], before, width
        self.n_dp, self.n_z, self.each = array.shape[0], array.shape[1], rows * width // array.shape[3]
        self.rows = self.n_dp * rows

    def specs(self):
        columns = self.arrays[0].shape[3]
        at = self.before // self.each
        return [pl.BlockSpec((self.n_dp, self.n_z, self.each, columns), lambda j, p: (0, 0, at, 0))]

    def load(self, refs, places):
        times = self.arrays[0].shape[3] // self.width

        def block(k, r):
            held = refs[0][places[k], places[self.n_dp + r]]
            return jnp.concatenate([held[:, i * self.width : (i + 1) * self.width] for i in range(times)], axis=0)

        rows = [jnp.concatenate([block(k, r) for r in range(self.n_z)], axis=1) for k in range(self.n_dp)]
        return jnp.concatenate(rows, axis=0)


def rows_times(places, x, weight, columns, tile, finish, extra, outs, name, chunks=1):
    length, depth = x.shape
    count = len(weight.arrays)

    def kernel(places_ref, x_ref, *refs):
        w = weight.load(refs[:count], places_ref)
        for low in range(0, tile, tile // chunks):
            cols = slice(low, low + tile // chunks)
            done = finish(dot(x_ref[...], w[:, cols]), *(r[:, cols] for r in refs[count : count + len(extra)]))
            for ref, value in zip(refs[count + len(extra) :], done):
                ref[:, cols] = value

    tall = pl.BlockSpec((length, tile), lambda j, p: (0, j))
    return pl.pallas_call(
        kernel,
        grid_spec=pltpu.PrefetchScalarGridSpec(
            num_scalar_prefetch=1,
            grid=(columns // tile,),
            in_specs=[pl.BlockSpec((length, depth), lambda j, p: (0, 0))] + weight.specs() + [tall] * len(extra),
            out_specs=[tall] * len(outs),
        ),
        out_shape=[jax.ShapeDtypeStruct((length, columns), t) for t in outs],
        compiler_params=params(),
        cost_estimate=COST,
        name=name,
    )(places, x, *weight.arrays, *extra)


def rows_times_t(places, x, weight, tile, finish, by_row, mods, row_outs, sums, name, to_place=None):
    n_dp = weight.n_dp
    feature = weight.rows // n_dp
    aligned = to_place is not None and feature % 128 == 0
    const = (mods,) if to_place is None or aligned else (mods, to_place)
    length, depth = x.shape
    count, steps, chunk = len(weight.arrays), depth // tile, SPATIAL * 2
    n_by, n_const, n_out = len(by_row), len(const), len(row_outs)

    def kernel(places_ref, x_ref, *refs):
        parts = iter(refs)
        w_refs, by_refs, const_refs, out_refs = ([next(parts) for _ in range(n)] for n in (count, n_by, n_const, n_out))
        sum_ref = next(parts) if sums else None
        acc = next(parts)
        term = dot_nt(x_ref[...], weight.load(w_refs, places_ref))

        @pl.when(pl.program_id(0) == 0)
        def _():
            acc[...] = term

        @pl.when(pl.program_id(0) > 0)
        def _():
            acc[...] += term

        @pl.when(pl.program_id(0) == steps - 1)
        def _():
            totals = None
            for i in range(0, length, chunk):
                rows = slice(i, i + chunk)
                done, adds = finish(acc[rows], *(r[rows] for r in by_refs), const_refs[0][...])
                for ref, value in zip(out_refs, done):
                    if aligned:
                        for k in range(n_dp):
                            at = pl.multiple_of(places_ref[k] * feature, 128)
                            ref[rows, pl.ds(at, feature)] = value[:, k * feature : (k + 1) * feature]
                    else:
                        ref[rows] = value if to_place is None else dot_nt(value, const_refs[1][...]).astype(BF)
                adds = [jnp.sum(v, axis=0, keepdims=True) for v in adds]
                totals = adds if totals is None else [t + v for t, v in zip(totals, adds)]
            if sums:
                sum_ref[...] = jnp.concatenate(totals, axis=0)

    def full(shape, **how):
        return pl.BlockSpec(shape, lambda j, p: (0, 0), **how)

    shapes = [jax.ShapeDtypeStruct(s, t) for s, t in row_outs]
    if sums:
        shapes.append(jax.ShapeDtypeStruct((sums, weight.rows), F32))
    return pl.pallas_call(
        kernel,
        grid_spec=pltpu.PrefetchScalarGridSpec(
            num_scalar_prefetch=1,
            grid=(steps,),
            in_specs=[pl.BlockSpec((length, tile), lambda j, p: (0, j))]
            + weight.specs()
            + [full(v.shape, pipeline_mode=pl.Buffered(1)) for v in (*by_row, *const)],
            out_specs=[full(v.shape) for v in shapes],
            scratch_shapes=[pltpu.VMEM((length, weight.rows), F32)],
        ),
        out_shape=shapes,
        compiler_params=params(40),
        cost_estimate=COST,
        name=name,
    )(places, x, *weight.arrays, *by_row, *const)


def rows_against(x, y, tile, name, places=None, n_dp=1):
    length, depth = x.shape
    columns = y.shape[1]
    rows = depth // n_dp

    def kernel(places_ref, x_ref, y_ref, *refs):
        turned = refs[-1]

        @pl.when(pl.program_id(0) == 0)
        def _():
            turned[...] = x_ref[...].T

        result = dot(turned[...], y_ref[...]).astype(BF)
        if n_dp == 1:
            refs[0][...] = result[: depth // 2]
            refs[1][...] = result[depth // 2 :]
        else:
            for k in range(n_dp):
                refs[0][places_ref[k]] = result[k * rows : (k + 1) * rows]

    if n_dp == 1:
        shape = jax.ShapeDtypeStruct((depth // 2, columns), BF)
        half = pl.BlockSpec((depth // 2, tile), lambda j, p: (0, j))
        out_shape, out_specs = [shape, shape], [half, half]
        places = jnp.zeros((1,), jnp.int32)
    else:
        out_shape = jax.ShapeDtypeStruct((n_dp, rows, columns), BF)
        out_specs = pl.BlockSpec((n_dp, rows, tile), lambda j, p: (0, 0, j))
    return pl.pallas_call(
        kernel,
        grid_spec=pltpu.PrefetchScalarGridSpec(
            num_scalar_prefetch=1,
            grid=(columns // tile,),
            in_specs=[
                pl.BlockSpec((length, depth), lambda j, p: (0, 0)),
                pl.BlockSpec((length, tile), lambda j, p: (0, j)),
            ],
            out_specs=out_specs,
            scratch_shapes=[pltpu.VMEM((depth, length), BF)],
        ),
        out_shape=out_shape,
        compiler_params=params(),
        cost_estimate=COST,
        name=name,
    )(places, x, y)


def head_cols(kind, h, width):
    return slice(kind * width + h * HEAD_DIM, kind * width + (h + 1) * HEAD_DIM)


def attend_kernel(heads, count_ref, qkv_ref, bias_ref, att_ref, prob_ref):
    width = heads * HEAD_DIM
    scale = jnp.asarray(HEAD_DIM**-0.5, BF)
    key_at = lax.broadcasted_iota(jnp.int32, (WIN_LEN, WIN_LEN), 0)
    row_at = lax.broadcasted_iota(jnp.int32, (WIN_LEN, width), 0)
    att = [[] for _ in range(WINDOWS)]
    for h in range(heads):
        bias = jnp.concatenate(
            [
                jnp.concatenate([bias_ref[h, a - b + WIN_T - 1] for a in range(WIN_T)], axis=1)
                for b in range(WIN_T)
            ],
            axis=0,
        )
        for w in range(WINDOWS):
            live = (count_ref[0] - w * WIN_T) * SPATIAL
            rows = slice(w * WIN_LEN, (w + 1) * WIN_LEN)
            q = qkv_ref[rows, head_cols(0, h, width)] * scale
            k = qkv_ref[rows, head_cols(1, h, width)]
            v = qkv_ref[rows, head_cols(2, h, width)]
            scores = jnp.where(key_at < live, dot_nt(k, q) + bias, NEGATIVE)
            top = jnp.max(scores, axis=0, keepdims=True)
            expo = jnp.exp(scores - top)
            total = jnp.maximum(jnp.sum(expo, axis=0, keepdims=True), 1.0)
            probs = (expo * jnp.where(live > 0, 1.0 / total, 0.0)).astype(BF)
            prob_ref[w, h] = probs
            att[w].append(dot_tn(v, probs))
    for w in range(WINDOWS):
        live = (count_ref[0] - w * WIN_T) * SPATIAL
        whole = jnp.concatenate(att[w], axis=0).T
        att_ref[w * WIN_LEN : (w + 1) * WIN_LEN, :] = jnp.where(row_at < live, whole, 0.0).astype(BF)


def attend_back_kernel(heads, count_ref, qkv_ref, prob_ref, gatt_ref, gqkv_ref, diag_ref):
    width = heads * HEAD_DIM
    scale = jnp.asarray(HEAD_DIM**-0.5, BF)
    row_at = lax.broadcasted_iota(jnp.int32, (WIN_LEN, HEAD_DIM), 0)
    grad_q = [[] for _ in range(WINDOWS)]
    for h in range(heads):
        both = None
        for w in range(WINDOWS):
            live = (count_ref[0] - w * WIN_T) * SPATIAL
            rows = slice(w * WIN_LEN, (w + 1) * WIN_LEN)
            q = qkv_ref[rows, head_cols(0, h, width)] * scale
            k = qkv_ref[rows, head_cols(1, h, width)] * scale
            v = qkv_ref[rows, head_cols(2, h, width)]
            gatt = gatt_ref[rows, head_cols(0, h, width)]
            gatt = jnp.where(row_at < live, gatt, jnp.zeros_like(gatt))
            probs = prob_ref[w, h]
            full = probs.astype(F32)
            gqkv_ref[rows, head_cols(2, h, width)] = dot(probs, gatt).astype(BF)
            gprobs = dot_nt(v, gatt)
            inner = jnp.sum(full * gprobs, axis=0, keepdims=True)
            gscores = (full * (gprobs - inner)).astype(BF)
            gqkv_ref[rows, head_cols(1, h, width)] = dot(gscores, q).astype(BF)
            grad_q[w].append(dot_tn(k, gscores))
            wide = gscores.astype(F32)
            both = wide if both is None else both + wide
        blocks = [both[b * SPATIAL : (b + 1) * SPATIAL] for b in range(WIN_T)]
        for t in range(SPREAD):
            pairs = [(b, b + t - WIN_T + 1) for b in range(WIN_T) if 0 <= b + t - WIN_T + 1 < WIN_T]
            diag_ref[h, t] = functools.reduce(
                lambda x, y: x + y, [blocks[b][:, a * SPATIAL : (a + 1) * SPATIAL] for b, a in pairs]
            )
    for w in range(WINDOWS):
        whole = jnp.concatenate(grad_q[w], axis=0).T
        gqkv_ref[w * WIN_LEN : (w + 1) * WIN_LEN, 0:width] = whole.astype(BF)


def attend(count, qkv, bias, n_z):
    heads = bias.shape[0] // n_z
    width = heads * HEAD_DIM
    length = WINDOWS * WIN_LEN
    return pl.pallas_call(
        functools.partial(attend_kernel, heads),
        grid_spec=pltpu.PrefetchScalarGridSpec(
            num_scalar_prefetch=1,
            grid=(n_z,),
            in_specs=[
                pl.BlockSpec((length, 3 * width), lambda r, c: (0, r)),
                pl.BlockSpec((heads, SPREAD, SPATIAL, SPATIAL), lambda r, c: (r, 0, 0, 0)),
            ],
            out_specs=[
                pl.BlockSpec((length, width), lambda r, c: (0, r)),
                pl.BlockSpec((WINDOWS, heads, WIN_LEN, WIN_LEN), lambda r, c: (0, r, 0, 0)),
            ],
        ),
        out_shape=[
            jax.ShapeDtypeStruct((length, n_z * width), BF),
            jax.ShapeDtypeStruct((WINDOWS, n_z * heads, WIN_LEN, WIN_LEN), BF),
        ],
        compiler_params=params(),
        cost_estimate=COST,
        name="attend",
    )(count, qkv, bias)


def attend_back(count, qkv, probs, gatt, n_z):
    heads = probs.shape[1] // n_z
    width = heads * HEAD_DIM
    length = WINDOWS * WIN_LEN
    return pl.pallas_call(
        functools.partial(attend_back_kernel, heads),
        grid_spec=pltpu.PrefetchScalarGridSpec(
            num_scalar_prefetch=1,
            grid=(n_z,),
            in_specs=[
                pl.BlockSpec((length, 3 * width), lambda r, c: (0, r)),
                pl.BlockSpec((WINDOWS, heads, WIN_LEN, WIN_LEN), lambda r, c: (0, r, 0, 0)),
                pl.BlockSpec((length, width), lambda r, c: (0, r)),
            ],
            out_specs=[
                pl.BlockSpec((length, 3 * width), lambda r, c: (0, r)),
                pl.BlockSpec((heads, SPREAD, SPATIAL, SPATIAL), lambda r, c: (r, 0, 0, 0)),
            ],
        ),
        out_shape=[
            jax.ShapeDtypeStruct((length, n_z * 3 * width), BF),
            jax.ShapeDtypeStruct((n_z * heads, SPREAD, SPATIAL, SPATIAL), F32),
        ],
        compiler_params=params(),
        cost_estimate=COST,
        name="attend_back",
    )(count, qkv, probs, gatt)


def normalize(values):
    center = values - jnp.mean(values, axis=-1, keepdims=True)
    scale = lax.rsqrt(jnp.mean(center * center, axis=-1, keepdims=True) + EPSILON)
    return center * scale, scale


def norm_back(normed, inv_sigma, scale_row, grad):
    u = (1.0 + scale_row) * grad
    return (u - jnp.mean(u, axis=-1, keepdims=True) - normed * jnp.mean(u * normed, axis=-1, keepdims=True)) * inv_sigma


def after_attention(branch_a, resid, mods):
    middle = resid.astype(F32) + mods[2:3] * branch_a
    normed = (normalize(middle)[0] * (1.0 + mods[4:5]) + mods[3:4]).astype(BF)
    return (branch_a, middle, normed), ()


def after_mlp(branch_b, middle, grad_result, mods):
    return ((middle + mods[5:6] * branch_b).astype(BF),), (grad_result.astype(F32) * branch_b,)


def back_mlp(grad_nb, middle, branch_a, grad_result, mods):
    norm_b, inv_b = normalize(middle)
    grad_middle = grad_result.astype(F32) + norm_back(norm_b, inv_b, mods[4:5], grad_nb)
    return (
        (grad_middle, (grad_middle * mods[2:3]).astype(BF)),
        (grad_middle * branch_a, grad_nb, grad_nb * norm_b),
    )


def back_attention(grad_na, resid, grad_middle, mods):
    norm_a, inv_a = normalize(resid.astype(F32))
    grad_tokens = (grad_middle + norm_back(norm_a, inv_a, mods[1:2], grad_na)).astype(BF)
    return (grad_tokens,), (grad_na, grad_na * norm_a)


def gelu_and_slope(v):
    c = float(np.sqrt(2 / np.pi))
    square = v * v
    h = 0.5 + 0.5 * jnp.tanh(v * (c + (0.044715 * c) * square))
    slope = h + h * (1.0 - h) * (v * (2 * c + (6 * 0.044715 * c) * square))
    return (v * h).astype(BF), slope.astype(BF)


def body(
    n_dp, n_z, tokens, conditioning, frame_counts, w_qkv, w_out, w_up, w_down, w_ada, pos_table, cotangent
):
    micro, clip_dev, _, part, model = tokens.shape
    clips = micro * clip_dev
    assert clips == n_z and part * n_z == SPATIAL
    feature = model // n_dp
    qkv_tile, hidden_tile, out_tile = 3 * w_out.shape[1], w_up.shape[1], w_out.shape[1]
    d, z = lax.axis_index("dp"), lax.axis_index("tensor")
    count = lax.dynamic_slice_in_dim(frame_counts.reshape(clips), z, 1)

    order = jnp.asarray(dp_order(n_dp))[d & 1] ^ d
    source = (order[:, None] * feature + jnp.arange(feature)[None, :]).reshape(1, model)
    to_place = (jnp.arange(model)[:, None] == source).astype(BF)

    places = jnp.concatenate([order, (z - jnp.arange(n_z)) % n_z]).astype(jnp.int32)

    def placed(rows):
        return dot(rows, to_place).astype(BF)

    def unplaced(rows):
        return dot_nt(rows.astype(BF), to_place).astype(BF)

    place = jnp.arange(SPATIAL)
    place = (z - place // part) % n_z * part + place % part

    def for_clips(rows):
        rows = rows.reshape(clips, FRAMES, part, model)
        return [lax.dynamic_index_in_dim(rows, (z + r) % n_z, 0, False) for r in range(n_z)]

    def to_clip(parts):
        with jax.named_scope("tokens_in"):
            return shifted(parts, n_z, 1)

    def in_order(got):
        return placed(jnp.stack(got, axis=1).reshape(FRAMES * SPATIAL, model))

    def from_clip(rows):
        rows = rows.reshape(FRAMES, n_z, part, model)
        return [rows[:, r] for r in range(n_z)]

    def by_clip(got):
        whole_rows = jnp.zeros((clips, FRAMES, part, model), BF)
        for r in range(n_z):
            whole_rows = lax.dynamic_update_index_in_dim(whole_rows, got[r], (z + r) % n_z, 0)
        return whole_rows.reshape(tokens.shape)

    few = stages(n_dp) == 2

    def gather(name, shard, at_once=False):
        at_once = at_once and few
        return Chain("gather_" + name, gather_steps(n_dp, n_z, shard, at_once), 1 + (1 if at_once else stages(n_dp)))

    def sum_dp(name, halves, at_once=False):
        return Chain("scatter_" + name, scatter_steps(n_dp, n_z, halves, at_once), 1 + (1 if at_once else stages(n_dp)))

    def exchange(name, pieces, sign, first=(n_z // 2,)):
        return Chain(name, exchange_steps(pieces, n_z, sign, first), 2)

    def butterfly(name, value, axis, size):
        return Chain(name, butterfly_steps(value, axis, size), size.bit_length() - 1)

    def gathered(shard):
        return lax.all_gather(shard, ("dp", "tensor"), axis=0).reshape((n_dp, n_z) + shard.shape)

    times = hidden_tile // out_tile
    if feature % (16 * times) == 0:
        folded = jnp.concatenate(jnp.split(w_out, times, axis=0), axis=1)
        held = gathered(jnp.concatenate([w_up, folded], axis=0))
        wu, wo = Gathered(held, feature), Folded(held, feature, feature, out_tile)
    else:
        wu, wo = Gathered(gathered(w_up), feature), Folded(gathered(w_out), 0, feature, out_tile)

    def turned(blocks):
        return jnp.concatenate([lax.dynamic_slice_in_dim(blocks, (z - r) % n_z, 1) for r in range(n_z)], axis=0)

    cond_float = conditioning.astype(F32).reshape(clips, model)
    cond_act = jax.nn.silu(cond_float).astype(BF)
    cond_mine = lax.all_to_all(
        cond_act.reshape(clips, n_dp, feature).transpose(1, 0, 2), "dp", 0, 0, tiled=True
    ).reshape(n_dp * clips, feature)
    share = -(-pos_table.size // n_dp)
    table = jnp.pad(pos_table.reshape(-1), (0, share * n_dp - pos_table.size)).reshape(n_dp, share)
    table = jnp.broadcast_to(lax.dynamic_slice_in_dim(table, d, 1), (n_dp * n_z, share))
    mod_part = dot(cond_mine, w_ada)
    columns = mod_part.shape[1]
    mod_part = lax.all_to_all(jnp.concatenate([mod_part, table], axis=1), ("dp", "tensor"), 0, 0, tiled=True)
    blocks = shifted([w_qkv.reshape(feature, -1)] * n_z, n_z, 1)
    blocks, to_place, got_tokens, places, count, mod_part = slot(
        [], blocks, to_place, for_clips(tokens), places, count, mod_part
    )
    wa = gather("qkv", join(blocks, 1), True)
    table = mod_part[:, columns:].reshape(n_dp, n_z, share).transpose(1, 0, 2).reshape(n_z, -1)[:, : pos_table.size]
    mods = jnp.sum(mod_part[:, :columns].reshape(n_dp, n_z, -1), axis=0).reshape(6, model)
    mods = jnp.dot(mods, to_place.astype(F32), precision=HIGHEST)
    bias = with_layout_constraint(spread_bias(turned(table).reshape(-1, OFFSETS), place), Layout((0, 1, 2, 3)))
    got_tokens, bias, mods = slot([wa], to_clip(got_tokens), bias, mods)
    resid = in_order(got_tokens)
    normed_a = (normalize(resid.astype(F32))[0] * (1.0 + mods[1:2]) + mods[0:1]).astype(BF)
    normed_a, w_down = slot([wa], normed_a, w_down)
    rows_of = (FRAMES * SPATIAL, model)

    w_in = Pieces(whole(wa), qkv_tile, n_dp)
    qkv, = rows_times(places, normed_a, w_in, qkv_tile * n_z, qkv_tile, lambda v: (v.astype(BF),), (), (BF,), "qkv")
    blocks = shifted([w_down] * n_z, n_z, 1)
    attended, probs = attend(count, qkv, bias, n_z)
    qkv, blocks, attended, probs, got_cotangent = slot([], qkv, blocks, attended, probs, for_clips(cotangent))
    wd = gather("down", join(blocks, 1))
    got_cotangent = to_clip(got_cotangent)
    branch_a, middle, normed_b = rows_times_t(
        places, attended, wo, out_tile * n_z, after_attention, (resid,), mods,
        ((rows_of, F32), (rows_of, F32), (rows_of, BF)), 0, "out",
    )
    activ, slope = rows_times(places, normed_b, wu, hidden_tile * n_z, hidden_tile, gelu_and_slope, (), (BF, BF), "up", 4)
    activ, slope, got_cotangent = slot([wd], activ, slope, got_cotangent)
    grad_result = in_order(got_cotangent)
    grad_bb = (grad_result.astype(F32) * mods[5:6]).astype(BF)
    gd = rows_against(grad_bb, activ, hidden_tile, "grad_down")
    activ, slope, grad_bb, gd = slot([wd], activ, slope, grad_bb, gd)
    gd = sum_dp("down", gd)
    activ, slope, grad_bb = slot([wd, gd], activ, slope, grad_bb)
    wd = Pieces(whole(wd), hidden_tile, n_dp)

    grad_hidden, = rows_times(
        places, grad_bb, wd, hidden_tile * n_z, hidden_tile, lambda v, s: ((v * s.astype(F32)).astype(BF),), (slope,), (BF,),
        "grad_hidden",
    )
    gu = rows_against(normed_b, grad_hidden, hidden_tile, "grad_up")
    block_out, sums_mlp = rows_times_t(
        places, activ, wd, hidden_tile, after_mlp, (middle, grad_result), mods, ((rows_of, BF),), 1, "down", to_place
    )
    grad_hidden, gu, block_out = slot([gd], grad_hidden, gu, from_clip(block_out))
    gu = sum_dp("up", gu)
    out_rows = exchange("tokens_out", block_out, -1)
    grad_middle, grad_ba, sums_mid = rows_times_t(
        places, grad_hidden, wu, hidden_tile, back_mlp, (middle, branch_a, grad_result), mods,
        ((rows_of, F32), (rows_of, BF)), 3, "grad_normed_b",
    )
    grad_middle, grad_ba = slot([gd, gu, out_rows], grad_middle, grad_ba)
    down_rows = exchange("down_sum", whole(gd), -1)
    go = rows_against(grad_ba, attended, out_tile * n_z, "grad_out", places, n_dp)
    grad_att, = rows_times(
        places, grad_ba, wo, out_tile * n_z, out_tile * n_z, lambda v: (v.astype(BF),), (), (BF,), "grad_att"
    )
    grad_qkv, diag = attend_back(count, qkv, probs, grad_att, n_z)
    grad_qkv, diag, go = slot([gu, down_rows, out_rows], grad_qkv, diag, go)
    go = lax.psum_scatter(go.reshape(model, -1), "dp", scatter_dimension=0, tiled=True)
    gq = rows_against(normed_a, grad_qkv, qkv_tile, "grad_qkv")
    table = turned(fold_bias(diag, place).reshape(n_z, -1, OFFSETS))
    table = jnp.pad(table, ((0, 0), (0, 0), (0, -OFFSETS % n_dp)))
    table = table.reshape(n_z, -1, n_dp, table.shape[2] // n_dp).transpose(2, 0, 1, 3)
    table = table.reshape((n_dp * n_z,) + table.shape[2:])
    gq, grad_qkv, table = slot([gu, down_rows], gq, grad_qkv, table)
    gq = sum_dp("qkv", gq, few)
    up_rows = exchange("up_sum", whole(gu), -1)
    grad_tokens, sums_in = rows_times_t(
        places, grad_qkv, w_in, qkv_tile, back_attention, (resid, grad_middle), mods, ((rows_of, BF),), 2,
        "grad_normed_a", to_place,
    )
    up_rows.step()
    in_rows = exchange("tokens_out", from_clip(grad_tokens), -1)
    in_rows.step()
    sums_in, block_out = slot([gq, up_rows], sums_in, whole(out_rows))
    in_rows.step()
    gq.step()
    if few:
        gq.value[1], sums_in = lax.optimization_barrier((gq.value[1], sums_in))
    grad_mod = unplaced(jnp.concatenate([sums_in, sums_mid, sums_mlp], axis=0)).reshape(1, n_z, -1)
    grad_mod = jnp.broadcast_to(grad_mod, (n_dp,) + grad_mod.shape[1:]).reshape(n_dp * n_z, -1).astype(F32)
    small = jnp.concatenate([grad_mod, table.reshape(n_dp * n_z, -1)], axis=1)
    small = lax.all_to_all(small, ("dp", "tensor"), 0, 0, tiled=True)
    gq.value, small, grad_tokens, go = slot([], gq.value, small, in_rows.value, go)

    terms = whole(gq) if few else [jnp.concatenate(whole(gq), axis=1)]
    pairs = attention_parts(terms, go, n_z)
    pairs, small = lax.optimization_barrier((pairs, small))
    pairs = functools.reduce(lambda a, b: a + b, [p.astype(F32) for p in shifted(pairs, n_z, -1)])
    mod_cols = small[:, :columns].astype(BF)
    act_part = dot_nt(mod_cols, w_ada).reshape(n_dp, 1, -1)
    act_part = jnp.broadcast_to(act_part, (n_dp, n_z, act_part.shape[2])).reshape(n_dp * n_z, -1)
    table = jnp.sum(small[:, columns:], axis=0)
    table = jnp.broadcast_to(table[None], (n_dp * n_z, table.shape[0]))
    small = lax.all_to_all(jnp.concatenate([act_part, table], axis=1), ("dp", "tensor"), 0, 0, tiled=True)
    small = small.reshape(n_dp, n_z, -1)
    grad_act = jnp.sum(small[:, :, : clips * feature], axis=1).reshape(n_dp, clips, feature)
    grad_act = grad_act.transpose(1, 0, 2).reshape(clips, model)
    grad_cond = jax.vjp(jax.nn.silu, cond_float)[1](grad_act)[0].reshape(conditioning.shape)
    table = lax.dynamic_index_in_dim(small[:, :, clips * feature :], z, 1, False)
    table = table.reshape(n_dp, pos_table.shape[0], -1).transpose(1, 0, 2)
    grad_table = table.reshape(pos_table.shape[0], -1)[:, :OFFSETS]
    grad_ada = dot_tn(cond_mine, mod_cols)
    block_out, grad_tokens = by_clip(block_out), by_clip(grad_tokens)
    out_down, out_up = (
        functools.reduce(lambda a, b: a + b, [p.astype(F32) for p in whole(rows)]) for rows in (down_rows, up_rows)
    )
    return (
        block_out,
        grad_tokens,
        grad_cond,
        pairs[:, :qkv_tile].reshape(w_qkv.shape),
        pairs[:, qkv_tile:],
        out_up,
        out_down,
        grad_ada,
        grad_table,
    )


def solution(mesh):
    rows = P(None, "dp", None, "tensor", None)
    weight = P("dp", "tensor")
    qkv_weight = P("dp", None, "tensor")
    cond = P(None, "dp", None)
    table = P("tensor", None)
    return jax.shard_map(
        functools.partial(body, mesh.shape["dp"], mesh.shape["tensor"]),
        mesh=mesh,
        in_specs=(rows, cond, P(None, "dp"), qkv_weight, weight, weight, weight, weight, table, rows),
        out_specs=(rows, rows, cond, qkv_weight, weight, weight, weight, weight, table),
        check_vma=False,
    )
```

```python
import functools

import jax
import jax.numpy as jnp
import numpy as np
from jax import lax
from jax.experimental import pallas as pl
from jax.experimental.layout import Layout, with_layout_constraint
from jax.experimental.pallas import tpu as pltpu
from jax.sharding import PartitionSpec as P

HEAD_DIM = 64
WIN_T = 5
WIN_S = 8
FRAMES = 10
SPATIAL = 64
OFFSETS = 2025

EPSILON = 1e-06
NEGATIVE = -1e30
HIGHEST = lax.Precision.HIGHEST
BF = jnp.bfloat16
F32 = jnp.float32
WINDOWS = FRAMES // WIN_T
WIN_LEN = WIN_T * SPATIAL
SPREAD = 2 * WIN_T - 1
DIAG = SPREAD * SPATIAL
GROUPS = 4


def stage_bits(n_dp, core):
    bits = list(range(1, n_dp.bit_length() - 1))
    return bits if core == 0 else bits[::-1]


def stage_perm(n_dp, stage):
    return [(i, i ^ (1 << stage_bits(n_dp, i & 1)[stage])) for i in range(n_dp)]


def core_perm(n_dp):
    return [(i, i ^ 1) for i in range(n_dp)]


def ring(count, step):
    return [(i, (i + step) % count) for i in range(count)]


def stages(n_dp):
    return n_dp.bit_length() - 2


def dp_order(n_dp):
    half = n_dp // 2

    def mask(core, place):
        return sum(1 << b for t, b in enumerate(stage_bits(n_dp, core)) if place >> t & 1)

    return np.array(
        [[mask(c, k) for k in range(half)] + [1 ^ mask(1 - c, k) for k in range(half)] for c in (0, 1)],
        np.int32,
    )


def join(blocks, axis):
    return join_parts(blocks, axis, [blocks[0].shape[1]])[0]


def join_parts(blocks, axis, widths):
    rows, count = blocks[0].shape[0], len(blocks)

    def kernel(*refs):
        low = 0
        for out, width in zip(refs[count:], widths):
            for i, ref in enumerate(refs[:count]):
                if axis == 0:
                    out[i * rows : (i + 1) * rows, :] = ref[:, low : low + width]
                else:
                    out[:, i * width : (i + 1) * width] = ref[:, low : low + width]
            low += width

    shapes = [(rows * count, w) if axis == 0 else (rows, w * count) for w in widths]
    return pl.pallas_call(
        kernel,
        out_shape=[jax.ShapeDtypeStruct(s, blocks[0].dtype) for s in shapes],
        compiler_params=params(),
        cost_estimate=COST,
        name="join",
    )(*blocks)


def place_perm(n_dp, place):
    order = dp_order(n_dp)
    return [(i, i ^ int(order[i & 1, place])) for i in range(n_dp)]


def gather_steps(n_dp, n_z, rows, at_once):
    if at_once:
        rows = yield [rows] + [lax.ppermute(rows, "dp", place_perm(n_dp, k)) for k in range(1, n_dp // 2)]
    else:
        for t in range(stages(n_dp)):
            got = lax.ppermute(rows, "dp", stage_perm(n_dp, t))
            rows, got = yield rows, got
            rows = join([rows, got], 0) if t < stages(n_dp) - 1 else [rows, got]
    yield rows + [lax.ppermute(p, "dp", core_perm(n_dp)) for p in rows]


def add_low(first, *others):
    return functools.reduce(lambda a, b: a + b, [o.astype(F32) for o in others], first.astype(F32)).astype(BF)


def scatter_steps(n_dp, n_z, halves, at_once):
    keep, send = halves
    got = lax.ppermute(send, "dp", core_perm(n_dp))
    if at_once:
        count = n_dp // 2
        rows = keep.shape[0] // count
        mine = [add_low(keep[k * rows : (k + 1) * rows], got[k * rows : (k + 1) * rows]) for k in range(count)]
        sent = yield mine[1:]
        far = lax.ppermute(sent[-1], "dp", place_perm(n_dp, count - 1))
        terms = mine[:1] + [lax.ppermute(v, "dp", place_perm(n_dp, k + 1)) for k, v in enumerate(sent[:-1])] + [far]
    else:
        for t in range(stages(n_dp) - 1, -1, -1):
            rows = keep.shape[0] // 2
            send, = yield [add_low(keep[rows:], got[rows:])]
            keep = add_low(keep[:rows], got[:rows])
            got = lax.ppermute(send, "dp", stage_perm(n_dp, t))
        terms = [keep, got]
    if at_once:
        yield terms
        return
    width = terms[0].shape[1] // n_z
    yield [add_low(*(v[:, r * width : (r + 1) * width] for v in terms)) for r in range(n_z)]


def attention_parts(terms, beside, n_z):
    rows = beside.shape[0]
    wide, narrow = terms[0].shape[1] // n_z, beside.shape[1] // n_z

    def kernel(*refs):
        for r, out in enumerate(refs[-n_z:]):
            total = refs[0][:, r * wide : (r + 1) * wide].astype(F32)
            for ref in refs[1 : -n_z - 1]:
                total = total + ref[:, r * wide : (r + 1) * wide].astype(F32)
            out[:, :wide] = total.astype(BF)
            out[:, wide:] = refs[-n_z - 1][:, r * narrow : (r + 1) * narrow]

    return pl.pallas_call(
        kernel,
        out_shape=[jax.ShapeDtypeStruct((rows, wide + narrow), BF)] * n_z,
        compiler_params=params(),
        cost_estimate=COST,
        name="attention_parts",
    )(*terms, beside)


class Chain:
    def __init__(self, name, steps, total):
        self.name, self.steps, self.left, self.value = name, steps, total, None

    def step(self):
        with jax.named_scope(f"{self.name}_{self.left}_left"):
            self.value = self.steps.send(self.value)
        self.left -= 1


def slot(chains, *values, free=()):
    chains = [c for c in chains if c.left]
    for chain in chains + [c for c in free if c.left]:
        chain.step()
    held, values = lax.optimization_barrier(([c.value for c in chains], values))
    for chain, value in zip(chains, held):
        chain.value = value
    return values[0] if len(values) == 1 else values


def whole(chain):
    while chain.left:
        slot([chain])
    return chain.value


def shifted(pieces, n_z, sign):
    return [pieces[0]] + [lax.ppermute(pieces[r], "tensor", ring(n_z, sign * r)) for r in range(1, n_z)]


def exchange_steps(pieces, n_z, sign, first):
    pieces = list(pieces)
    for group in (first, [r for r in range(1, n_z) if r not in first]):
        for r in group:
            pieces[r] = lax.ppermute(pieces[r], "tensor", ring(n_z, sign * r))
        pieces = yield pieces


def butterfly_steps(value, axis, count):
    bit = 1
    while bit < count:
        value = yield value + lax.ppermute(value, axis, [(i, i ^ bit) for i in range(count)])
        bit *= 2


def pair_onehot(place):
    span = 2 * WIN_S - 1
    row, col = place // WIN_S, place % WIN_S
    offset = (row[None, :] - row[:, None] + WIN_S - 1) * span + (col[None, :] - col[:, None] + WIN_S - 1)
    return (jnp.arange(span * span)[:, None] == offset.reshape(1, -1)).astype(F32)


def spread_bias(table, place):
    heads = table.shape[0]
    flat = jnp.dot(table.reshape(heads * SPREAD, -1), pair_onehot(place), precision=HIGHEST)
    return flat.reshape(heads, SPREAD, SPATIAL, SPATIAL)


def fold_bias(diag, place):
    heads = diag.shape[0]
    rows = diag.reshape(heads * SPREAD, SPATIAL * SPATIAL)
    folded = lax.dot_general(rows, pair_onehot(place), (((1,), (1,)), ((), ())), precision=HIGHEST)
    return folded.reshape(heads, OFFSETS)


def dot(a, b):
    return jnp.dot(a, b, preferred_element_type=F32)


def dot_nt(a, b):
    return lax.dot_general(a, b, (((1,), (1,)), ((), ())), preferred_element_type=F32)


def dot_tn(a, b):
    return lax.dot_general(a, b, (((0,), (0,)), ((), ())), preferred_element_type=F32)


def params(mib=28):
    return pltpu.CompilerParams(vmem_limit_bytes=mib << 20)


COST = pl.CostEstimate(flops=10**6, bytes_accessed=10**4, transcendentals=0)


class Pieces:
    def __init__(self, arrays, width, n_dp):
        self.arrays, self.width, self.n_dp = arrays, width, n_dp
        self.rows = sum(a.shape[0] for a in arrays)

    def specs(self):
        return [pl.BlockSpec((a.shape[0], self.width), lambda j, p: (0, j)) for a in self.arrays]

    def load(self, refs, places):
        return jnp.concatenate([r[...] for r in refs], axis=0)


class Gathered:
    def __init__(self, array, rows):
        self.arrays, self.each, self.n_dp = [array], rows, array.shape[0]
        self.rows = self.n_dp * rows

    def specs(self):
        n_dp, _, _, columns = self.arrays[0].shape
        return [pl.BlockSpec((n_dp, 1, self.each, columns), lambda j, p: (0, p[n_dp + j], 0, 0))]

    def load(self, refs, places):
        return jnp.concatenate([refs[0][places[k], 0] for k in range(self.n_dp)], axis=0)


class Folded:
    def __init__(self, array, before, rows, width):
        self.arrays, self.before, self.width = [array], before, width
        self.n_dp, self.n_z, self.each = array.shape[0], array.shape[1], rows * width // array.shape[3]
        self.rows = self.n_dp * rows

    def specs(self):
        columns = self.arrays[0].shape[3]
        at = self.before // self.each
        return [pl.BlockSpec((self.n_dp, self.n_z, self.each, columns), lambda j, p: (0, 0, at, 0))]

    def load(self, refs, places):
        times = self.arrays[0].shape[3] // self.width

        def block(k, r):
            held = refs[0][places[k], places[self.n_dp + r]]
            return jnp.concatenate([held[:, i * self.width : (i + 1) * self.width] for i in range(times)], axis=0)

        rows = [jnp.concatenate([block(k, r) for r in range(self.n_z)], axis=1) for k in range(self.n_dp)]
        return jnp.concatenate(rows, axis=0)


def rows_times(places, x, weight, columns, tile, finish, extra, outs, name, chunks=1):
    length, depth = x.shape
    count = len(weight.arrays)

    def kernel(places_ref, x_ref, *refs):
        w = weight.load(refs[:count], places_ref)
        for low in range(0, tile, tile // chunks):
            cols = slice(low, low + tile // chunks)
            done = finish(dot(x_ref[...], w[:, cols]), *(r[:, cols] for r in refs[count : count + len(extra)]))
            for ref, value in zip(refs[count + len(extra) :], done):
                ref[:, cols] = value

    tall = pl.BlockSpec((length, tile), lambda j, p: (0, j))
    return pl.pallas_call(
        kernel,
        grid_spec=pltpu.PrefetchScalarGridSpec(
            num_scalar_prefetch=1,
            grid=(columns // tile,),
            in_specs=[pl.BlockSpec((length, depth), lambda j, p: (0, 0))] + weight.specs() + [tall] * len(extra),
            out_specs=[tall] * len(outs),
        ),
        out_shape=[jax.ShapeDtypeStruct((length, columns), t) for t in outs],
        compiler_params=params(),
        cost_estimate=COST,
        name=name,
    )(places, x, *weight.arrays, *extra)


def rows_times_t(places, x, weight, tile, finish, by_row, mods, row_outs, sums, name, to_place=None):
    n_dp = weight.n_dp
    feature = weight.rows // n_dp
    aligned = to_place is not None and feature % 128 == 0
    const = (mods,) if to_place is None or aligned else (mods, to_place)
    length, depth = x.shape
    count, steps, chunk = len(weight.arrays), depth // tile, SPATIAL * 2
    n_by, n_const, n_out = len(by_row), len(const), len(row_outs)

    def kernel(places_ref, x_ref, *refs):
        parts = iter(refs)
        w_refs, by_refs, const_refs, out_refs = ([next(parts) for _ in range(n)] for n in (count, n_by, n_const, n_out))
        sum_ref = next(parts) if sums else None
        acc = next(parts)
        term = dot_nt(x_ref[...], weight.load(w_refs, places_ref))

        @pl.when(pl.program_id(0) == 0)
        def _():
            acc[...] = term

        @pl.when(pl.program_id(0) > 0)
        def _():
            acc[...] += term

        @pl.when(pl.program_id(0) == steps - 1)
        def _():
            totals = None
            for i in range(0, length, chunk):
                rows = slice(i, i + chunk)
                done, adds = finish(acc[rows], *(r[rows] for r in by_refs), const_refs[0][...])
                for ref, value in zip(out_refs, done):
                    if aligned:
                        for k in range(n_dp):
                            at = pl.multiple_of(places_ref[k] * feature, 128)
                            ref[rows, pl.ds(at, feature)] = value[:, k * feature : (k + 1) * feature]
                    else:
                        ref[rows] = value if to_place is None else dot_nt(value, const_refs[1][...]).astype(BF)
                adds = [jnp.sum(v, axis=0, keepdims=True) for v in adds]
                totals = adds if totals is None else [t + v for t, v in zip(totals, adds)]
            if sums:
                sum_ref[...] = jnp.concatenate(totals, axis=0)

    def full(shape, **how):
        return pl.BlockSpec(shape, lambda j, p: (0, 0), **how)

    shapes = [jax.ShapeDtypeStruct(s, t) for s, t in row_outs]
    if sums:
        shapes.append(jax.ShapeDtypeStruct((sums, weight.rows), F32))
    return pl.pallas_call(
        kernel,
        grid_spec=pltpu.PrefetchScalarGridSpec(
            num_scalar_prefetch=1,
            grid=(steps,),
            in_specs=[pl.BlockSpec((length, tile), lambda j, p: (0, j))]
            + weight.specs()
            + [full(v.shape, pipeline_mode=pl.Buffered(1)) for v in (*by_row, *const)],
            out_specs=[full(v.shape) for v in shapes],
            scratch_shapes=[pltpu.VMEM((length, weight.rows), F32)],
        ),
        out_shape=shapes,
        compiler_params=params(40),
        cost_estimate=COST,
        name=name,
    )(places, x, *weight.arrays, *by_row, *const)


def rows_against(x, y, tile, name, places=None, n_dp=1):
    length, depth = x.shape
    columns = y.shape[1]
    rows = depth // n_dp

    def kernel(places_ref, x_ref, y_ref, *refs):
        turned = refs[-1]

        @pl.when(pl.program_id(0) == 0)
        def _():
            turned[...] = x_ref[...].T

        result = dot(turned[...], y_ref[...]).astype(BF)
        if n_dp == 1:
            refs[0][...] = result[: depth // 2]
            refs[1][...] = result[depth // 2 :]
        else:
            for k in range(n_dp):
                refs[0][places_ref[k]] = result[k * rows : (k + 1) * rows]

    if n_dp == 1:
        shape = jax.ShapeDtypeStruct((depth // 2, columns), BF)
        half = pl.BlockSpec((depth // 2, tile), lambda j, p: (0, j))
        out_shape, out_specs = [shape, shape], [half, half]
        places = jnp.zeros((1,), jnp.int32)
    else:
        out_shape = jax.ShapeDtypeStruct((n_dp, rows, columns), BF)
        out_specs = pl.BlockSpec((n_dp, rows, tile), lambda j, p: (0, 0, j))
    return pl.pallas_call(
        kernel,
        grid_spec=pltpu.PrefetchScalarGridSpec(
            num_scalar_prefetch=1,
            grid=(columns // tile,),
            in_specs=[
                pl.BlockSpec((length, depth), lambda j, p: (0, 0)),
                pl.BlockSpec((length, tile), lambda j, p: (0, j)),
            ],
            out_specs=out_specs,
            scratch_shapes=[pltpu.VMEM((depth, length), BF)],
        ),
        out_shape=out_shape,
        compiler_params=params(),
        cost_estimate=COST,
        name=name,
    )(places, x, y)


def head_cols(kind, h, width):
    return slice(kind * width + h * HEAD_DIM, kind * width + (h + 1) * HEAD_DIM)


def attend_kernel(heads, count_ref, qkv_ref, bias_ref, att_ref, prob_ref):
    width = heads * HEAD_DIM
    scale = jnp.asarray(HEAD_DIM**-0.5, BF)
    key_at = lax.broadcasted_iota(jnp.int32, (WIN_LEN, WIN_LEN), 0)
    row_at = lax.broadcasted_iota(jnp.int32, (WIN_LEN, width), 0)
    att = [[] for _ in range(WINDOWS)]
    for h in range(heads):
        bias = jnp.concatenate(
            [
                jnp.concatenate([bias_ref[h, a - b + WIN_T - 1] for a in range(WIN_T)], axis=1)
                for b in range(WIN_T)
            ],
            axis=0,
        )
        for w in range(WINDOWS):
            live = (count_ref[0] - w * WIN_T) * SPATIAL
            rows = slice(w * WIN_LEN, (w + 1) * WIN_LEN)
            q = qkv_ref[rows, head_cols(0, h, width)] * scale
            k = qkv_ref[rows, head_cols(1, h, width)]
            v = qkv_ref[rows, head_cols(2, h, width)]
            scores = jnp.where(key_at < live, dot_nt(k, q) + bias, NEGATIVE)
            top = jnp.max(scores, axis=0, keepdims=True)
            expo = jnp.exp(scores - top)
            total = jnp.maximum(jnp.sum(expo, axis=0, keepdims=True), 1.0)
            probs = (expo * jnp.where(live > 0, 1.0 / total, 0.0)).astype(BF)
            prob_ref[w, h] = probs
            att[w].append(dot_tn(v, probs))
    for w in range(WINDOWS):
        live = (count_ref[0] - w * WIN_T) * SPATIAL
        whole = jnp.concatenate(att[w], axis=0).T
        att_ref[w * WIN_LEN : (w + 1) * WIN_LEN, :] = jnp.where(row_at < live, whole, 0.0).astype(BF)


def attend_back_kernel(heads, count_ref, qkv_ref, prob_ref, gatt_ref, gqkv_ref, diag_ref):
    width = heads * HEAD_DIM
    scale = jnp.asarray(HEAD_DIM**-0.5, BF)
    row_at = lax.broadcasted_iota(jnp.int32, (WIN_LEN, HEAD_DIM), 0)
    grad_q = [[] for _ in range(WINDOWS)]
    for h in range(heads):
        both = None
        for w in range(WINDOWS):
            live = (count_ref[0] - w * WIN_T) * SPATIAL
            rows = slice(w * WIN_LEN, (w + 1) * WIN_LEN)
            q = qkv_ref[rows, head_cols(0, h, width)] * scale
            k = qkv_ref[rows, head_cols(1, h, width)] * scale
            v = qkv_ref[rows, head_cols(2, h, width)]
            gatt = gatt_ref[rows, head_cols(0, h, width)]
            gatt = jnp.where(row_at < live, gatt, jnp.zeros_like(gatt))
            probs = prob_ref[w, h]
            full = probs.astype(F32)
            gqkv_ref[rows, head_cols(2, h, width)] = dot(probs, gatt).astype(BF)
            gprobs = dot_nt(v, gatt)
            inner = jnp.sum(full * gprobs, axis=0, keepdims=True)
            gscores = (full * (gprobs - inner)).astype(BF)
            gqkv_ref[rows, head_cols(1, h, width)] = dot(gscores, q).astype(BF)
            grad_q[w].append(dot_tn(k, gscores))
            wide = gscores.astype(F32)
            both = wide if both is None else both + wide
        blocks = [both[b * SPATIAL : (b + 1) * SPATIAL] for b in range(WIN_T)]
        for t in range(SPREAD):
            pairs = [(b, b + t - WIN_T + 1) for b in range(WIN_T) if 0 <= b + t - WIN_T + 1 < WIN_T]
            diag_ref[h, t] = functools.reduce(
                lambda x, y: x + y, [blocks[b][:, a * SPATIAL : (a + 1) * SPATIAL] for b, a in pairs]
            )
    for w in range(WINDOWS):
        whole = jnp.concatenate(grad_q[w], axis=0).T
        gqkv_ref[w * WIN_LEN : (w + 1) * WIN_LEN, 0:width] = whole.astype(BF)


def attend(count, qkv, bias, n_z):
    heads = bias.shape[0] // n_z
    width = heads * HEAD_DIM
    length = WINDOWS * WIN_LEN
    return pl.pallas_call(
        functools.partial(attend_kernel, heads),
        grid_spec=pltpu.PrefetchScalarGridSpec(
            num_scalar_prefetch=1,
            grid=(n_z,),
            in_specs=[
                pl.BlockSpec((length, 3 * width), lambda r, c: (0, r)),
                pl.BlockSpec((heads, SPREAD, SPATIAL, SPATIAL), lambda r, c: (r, 0, 0, 0)),
            ],
            out_specs=[
                pl.BlockSpec((length, width), lambda r, c: (0, r)),
                pl.BlockSpec((WINDOWS, heads, WIN_LEN, WIN_LEN), lambda r, c: (0, r, 0, 0)),
            ],
        ),
        out_shape=[
            jax.ShapeDtypeStruct((length, n_z * width), BF),
            jax.ShapeDtypeStruct((WINDOWS, n_z * heads, WIN_LEN, WIN_LEN), BF),
        ],
        compiler_params=params(),
        cost_estimate=COST,
        name="attend",
    )(count, qkv, bias)


def attend_back(count, qkv, probs, gatt, n_z):
    heads = probs.shape[1] // n_z
    width = heads * HEAD_DIM
    length = WINDOWS * WIN_LEN
    return pl.pallas_call(
        functools.partial(attend_back_kernel, heads),
        grid_spec=pltpu.PrefetchScalarGridSpec(
            num_scalar_prefetch=1,
            grid=(n_z,),
            in_specs=[
                pl.BlockSpec((length, 3 * width), lambda r, c: (0, r)),
                pl.BlockSpec((WINDOWS, heads, WIN_LEN, WIN_LEN), lambda r, c: (0, r, 0, 0)),
                pl.BlockSpec((length, width), lambda r, c: (0, r)),
            ],
            out_specs=[
                pl.BlockSpec((length, 3 * width), lambda r, c: (0, r)),
                pl.BlockSpec((heads, SPREAD, SPATIAL, SPATIAL), lambda r, c: (r, 0, 0, 0)),
            ],
        ),
        out_shape=[
            jax.ShapeDtypeStruct((length, n_z * 3 * width), BF),
            jax.ShapeDtypeStruct((n_z * heads, SPREAD, SPATIAL, SPATIAL), F32),
        ],
        compiler_params=params(),
        cost_estimate=COST,
        name="attend_back",
    )(count, qkv, probs, gatt)


def normalize(values):
    center = values - jnp.mean(values, axis=-1, keepdims=True)
    scale = lax.rsqrt(jnp.mean(center * center, axis=-1, keepdims=True) + EPSILON)
    return center * scale, scale


def norm_back(normed, inv_sigma, scale_row, grad):
    u = (1.0 + scale_row) * grad
    return (u - jnp.mean(u, axis=-1, keepdims=True) - normed * jnp.mean(u * normed, axis=-1, keepdims=True)) * inv_sigma


def after_attention(branch_a, resid, mods):
    middle = resid.astype(F32) + mods[2:3] * branch_a
    normed = (normalize(middle)[0] * (1.0 + mods[4:5]) + mods[3:4]).astype(BF)
    return (branch_a, middle, normed), ()


def after_mlp(branch_b, middle, grad_result, mods):
    return ((middle + mods[5:6] * branch_b).astype(BF),), (grad_result.astype(F32) * branch_b,)


def back_mlp(grad_nb, middle, branch_a, grad_result, mods):
    norm_b, inv_b = normalize(middle)
    grad_middle = grad_result.astype(F32) + norm_back(norm_b, inv_b, mods[4:5], grad_nb)
    return (
        (grad_middle, (grad_middle * mods[2:3]).astype(BF)),
        (grad_middle * branch_a, grad_nb, grad_nb * norm_b),
    )


def back_attention(grad_na, resid, grad_middle, mods):
    norm_a, inv_a = normalize(resid.astype(F32))
    grad_tokens = (grad_middle + norm_back(norm_a, inv_a, mods[1:2], grad_na)).astype(BF)
    return (grad_tokens,), (grad_na, grad_na * norm_a)


def gelu_and_slope(v):
    c = float(np.sqrt(2 / np.pi))
    square = v * v
    h = 0.5 + 0.5 * jnp.tanh(v * (c + (0.044715 * c) * square))
    slope = h + h * (1.0 - h) * (v * (2 * c + (6 * 0.044715 * c) * square))
    return (v * h).astype(BF), slope.astype(BF)


def body(
    n_dp, n_z, tokens, conditioning, frame_counts, w_qkv, w_out, w_up, w_down, w_ada, pos_table, cotangent
):
    micro, clip_dev, _, part, model = tokens.shape
    clips = micro * clip_dev
    assert clips == n_z and part * n_z == SPATIAL
    feature = model // n_dp
    qkv_tile, hidden_tile, out_tile = 3 * w_out.shape[1], w_up.shape[1], w_out.shape[1]
    d, z = lax.axis_index("dp"), lax.axis_index("tensor")
    count = lax.dynamic_slice_in_dim(frame_counts.reshape(clips), z, 1)

    order = jnp.asarray(dp_order(n_dp))[d & 1] ^ d
    source = (order[:, None] * feature + jnp.arange(feature)[None, :]).reshape(1, model)
    to_place = (jnp.arange(model)[:, None] == source).astype(BF)

    places = jnp.concatenate([order, (z - jnp.arange(n_z)) % n_z]).astype(jnp.int32)

    def placed(rows):
        return dot(rows, to_place).astype(BF)

    def unplaced(rows):
        return dot_nt(rows.astype(BF), to_place).astype(BF)

    place = jnp.arange(SPATIAL)
    place = (z - place // part) % n_z * part + place % part

    def for_clips(rows):
        rows = rows.reshape(clips, FRAMES, part, model)
        return [lax.dynamic_index_in_dim(rows, (z + r) % n_z, 0, False) for r in range(n_z)]

    def to_clip(parts):
        with jax.named_scope("tokens_in"):
            return shifted(parts, n_z, 1)

    def in_order(got):
        return placed(jnp.stack(got, axis=1).reshape(FRAMES * SPATIAL, model))

    def from_clip(rows):
        rows = rows.reshape(FRAMES, n_z, part, model)
        return [rows[:, r] for r in range(n_z)]

    def by_clip(got):
        whole_rows = jnp.zeros((clips, FRAMES, part, model), BF)
        for r in range(n_z):
            whole_rows = lax.dynamic_update_index_in_dim(whole_rows, got[r], (z + r) % n_z, 0)
        return whole_rows.reshape(tokens.shape)

    few = stages(n_dp) == 2

    def gather(name, shard, at_once=False):
        at_once = at_once and few
        return Chain("gather_" + name, gather_steps(n_dp, n_z, shard, at_once), 1 + (1 if at_once else stages(n_dp)))

    def sum_dp(name, halves, at_once=False):
        return Chain("scatter_" + name, scatter_steps(n_dp, n_z, halves, at_once), 1 + (1 if at_once else stages(n_dp)))

    def exchange(name, pieces, sign, first=(n_z // 2,)):
        return Chain(name, exchange_steps(pieces, n_z, sign, first), 2)

    def butterfly(name, value, axis, size):
        return Chain(name, butterfly_steps(value, axis, size), size.bit_length() - 1)

    def gathered(shard):
        return lax.all_gather(shard, ("dp", "tensor"), axis=0).reshape((n_dp, n_z) + shard.shape)

    times = hidden_tile // out_tile
    if feature % (16 * times) == 0:
        folded = jnp.concatenate(jnp.split(w_out, times, axis=0), axis=1)
        held = gathered(jnp.concatenate([w_up, folded], axis=0))
        wu, wo = Gathered(held, feature), Folded(held, feature, feature, out_tile)
    else:
        wu, wo = Gathered(gathered(w_up), feature), Folded(gathered(w_out), 0, feature, out_tile)

    def turned(blocks):
        return jnp.concatenate([lax.dynamic_slice_in_dim(blocks, (z - r) % n_z, 1) for r in range(n_z)], axis=0)

    cond_float = conditioning.astype(F32).reshape(clips, model)
    cond_act = jax.nn.silu(cond_float).astype(BF)
    cond_mine = lax.all_to_all(
        cond_act.reshape(clips, n_dp, feature).transpose(1, 0, 2), "dp", 0, 0, tiled=True
    ).reshape(n_dp * clips, feature)
    share = -(-pos_table.size // n_dp)
    table = jnp.pad(pos_table.reshape(-1), (0, share * n_dp - pos_table.size)).reshape(n_dp, share)
    table = jnp.broadcast_to(lax.dynamic_slice_in_dim(table, d, 1), (n_dp * n_z, share))
    mod_part = dot(cond_mine, w_ada)
    columns = mod_part.shape[1]
    mod_part = lax.all_to_all(jnp.concatenate([mod_part, table], axis=1), ("dp", "tensor"), 0, 0, tiled=True)
    blocks = shifted([w_qkv.reshape(feature, -1)] * n_z, n_z, 1)
    blocks, to_place, got_tokens, places, count, mod_part = slot(
        [], blocks, to_place, for_clips(tokens), places, count, mod_part
    )
    wa = gather("qkv", join(blocks, 1), True)
    table = mod_part[:, columns:].reshape(n_dp, n_z, share).transpose(1, 0, 2).reshape(n_z, -1)[:, : pos_table.size]
    mods = jnp.sum(mod_part[:, :columns].reshape(n_dp, n_z, -1), axis=0).reshape(6, model)
    mods = jnp.dot(mods, to_place.astype(F32), precision=HIGHEST)
    bias = with_layout_constraint(spread_bias(turned(table).reshape(-1, OFFSETS), place), Layout((0, 1, 2, 3)))
    got_tokens, bias, mods = slot([wa], to_clip(got_tokens), bias, mods)
    resid = in_order(got_tokens)
    normed_a = (normalize(resid.astype(F32))[0] * (1.0 + mods[1:2]) + mods[0:1]).astype(BF)
    normed_a, w_down = slot([wa], normed_a, w_down)
    rows_of = (FRAMES * SPATIAL, model)

    w_in = Pieces(whole(wa), qkv_tile, n_dp)
    qkv, = rows_times(places, normed_a, w_in, qkv_tile * n_z, qkv_tile, lambda v: (v.astype(BF),), (), (BF,), "qkv")
    blocks = shifted([w_down] * n_z, n_z, 1)
    attended, probs = attend(count, qkv, bias, n_z)
    qkv, blocks, attended, probs, got_cotangent = slot([], qkv, blocks, attended, probs, for_clips(cotangent))
    wd = gather("down", join(blocks, 1))
    cot_rows = exchange("tokens_in", got_cotangent, 1)
    branch_a, middle, normed_b = rows_times_t(
        places, attended, wo, out_tile * n_z, after_attention, (resid,), mods,
        ((rows_of, F32), (rows_of, F32), (rows_of, BF)), 0, "out",
    )
    branch_a, middle, normed_b = slot([wd, cot_rows], branch_a, middle, normed_b)
    activ, slope = rows_times(places, normed_b, wu, hidden_tile * n_z, hidden_tile, gelu_and_slope, (), (BF, BF), "up", 4)
    cot_rows.step()
    grad_result = in_order(cot_rows.value)
    grad_bb = (grad_result.astype(F32) * mods[5:6]).astype(BF)
    activ, slope, grad_bb = slot([wd], activ, slope, grad_bb)
    gd = rows_against(grad_bb, activ, hidden_tile, "grad_down")
    activ, slope, grad_bb, gd = slot([wd], activ, slope, grad_bb, gd)
    gd = sum_dp("down", gd)
    wd = Pieces(whole(wd), hidden_tile, n_dp)

    grad_hidden, = rows_times(
        places, grad_bb, wd, hidden_tile * n_z, hidden_tile, lambda v, s: ((v * s.astype(F32)).astype(BF),), (slope,), (BF,),
        "grad_hidden",
    )
    grad_hidden, activ = slot([gd], grad_hidden, activ)
    gu = rows_against(normed_b, grad_hidden, hidden_tile, "grad_up")
    block_out, sums_mlp = rows_times_t(
        places, activ, wd, hidden_tile, after_mlp, (middle, grad_result), mods, ((rows_of, BF),), 1, "down", to_place
    )
    grad_hidden, gu, block_out = slot([gd], grad_hidden, gu, from_clip(block_out))
    gu = sum_dp("up", gu)
    out_rows = exchange("tokens_out", block_out, -1)
    grad_middle, grad_ba, sums_mid = rows_times_t(
        places, grad_hidden, wu, hidden_tile, back_mlp, (middle, branch_a, grad_result), mods,
        ((rows_of, F32), (rows_of, BF)), 3, "grad_normed_b",
    )
    grad_middle, grad_ba = slot([gd, gu, out_rows], grad_middle, grad_ba)
    down_rows = exchange("down_sum", whole(gd), -1)
    go = rows_against(grad_ba, attended, out_tile * n_z, "grad_out", places, n_dp)
    grad_att, = rows_times(
        places, grad_ba, wo, out_tile * n_z, out_tile * n_z, lambda v: (v.astype(BF),), (), (BF,), "grad_att"
    )
    grad_qkv, diag = attend_back(count, qkv, probs, grad_att, n_z)
    grad_qkv, diag, go = slot([gu, down_rows, out_rows], grad_qkv, diag, go)
    go = lax.psum_scatter(go.reshape(model, -1), "dp", scatter_dimension=0, tiled=True)
    gq = rows_against(normed_a, grad_qkv, qkv_tile, "grad_qkv")
    table = turned(fold_bias(diag, place).reshape(n_z, -1, OFFSETS))
    table = jnp.pad(table, ((0, 0), (0, 0), (0, -OFFSETS % n_dp)))
    table = table.reshape(n_z, -1, n_dp, table.shape[2] // n_dp).transpose(2, 0, 1, 3)
    table = table.reshape((n_dp * n_z,) + table.shape[2:])
    gq, grad_qkv, table = slot([gu, down_rows], gq, grad_qkv, table)
    gq = sum_dp("qkv", gq, few)
    up_rows = exchange("up_sum", whole(gu), -1)
    grad_tokens, sums_in = rows_times_t(
        places, grad_qkv, w_in, qkv_tile, back_attention, (resid, grad_middle), mods, ((rows_of, BF),), 2,
        "grad_normed_a", to_place,
    )
    up_rows.step()
    in_rows = exchange("tokens_out", from_clip(grad_tokens), -1)
    in_rows.step()
    sums_in, block_out = slot([gq, up_rows], sums_in, whole(out_rows))
    in_rows.step()
    gq.step()
    if few:
        gq.value[1], sums_in = lax.optimization_barrier((gq.value[1], sums_in))
    grad_mod = unplaced(jnp.concatenate([sums_in, sums_mid, sums_mlp], axis=0)).reshape(1, n_z, -1)
    grad_mod = jnp.broadcast_to(grad_mod, (n_dp,) + grad_mod.shape[1:]).reshape(n_dp * n_z, -1).astype(F32)
    small = jnp.concatenate([grad_mod, table.reshape(n_dp * n_z, -1)], axis=1)
    small = lax.all_to_all(small, ("dp", "tensor"), 0, 0, tiled=True)
    gq.value, small, grad_tokens, go = slot([], gq.value, small, in_rows.value, go)

    terms = whole(gq) if few else [jnp.concatenate(whole(gq), axis=1)]
    pairs = attention_parts(terms, go, n_z)
    pairs, small = lax.optimization_barrier((pairs, small))
    pairs = functools.reduce(lambda a, b: a + b, [p.astype(F32) for p in shifted(pairs, n_z, -1)])
    mod_cols = small[:, :columns].astype(BF)
    act_part = dot_nt(mod_cols, w_ada).reshape(n_dp, 1, -1)
    act_part = jnp.broadcast_to(act_part, (n_dp, n_z, act_part.shape[2])).reshape(n_dp * n_z, -1)
    table = jnp.sum(small[:, columns:], axis=0)
    table = jnp.broadcast_to(table[None], (n_dp * n_z, table.shape[0]))
    small = lax.all_to_all(jnp.concatenate([act_part, table], axis=1), ("dp", "tensor"), 0, 0, tiled=True)
    small = small.reshape(n_dp, n_z, -1)
    grad_act = jnp.sum(small[:, :, : clips * feature], axis=1).reshape(n_dp, clips, feature)
    grad_act = grad_act.transpose(1, 0, 2).reshape(clips, model)
    grad_cond = jax.vjp(jax.nn.silu, cond_float)[1](grad_act)[0].reshape(conditioning.shape)
    table = lax.dynamic_index_in_dim(small[:, :, clips * feature :], z, 1, False)
    table = table.reshape(n_dp, pos_table.shape[0], -1).transpose(1, 0, 2)
    grad_table = table.reshape(pos_table.shape[0], -1)[:, :OFFSETS]
    grad_ada = dot_tn(cond_mine, mod_cols)
    block_out, grad_tokens = by_clip(block_out), by_clip(grad_tokens)
    out_down, out_up = (
        functools.reduce(lambda a, b: a + b, [p.astype(F32) for p in whole(rows)]) for rows in (down_rows, up_rows)
    )
    return (
        block_out,
        grad_tokens,
        grad_cond,
        pairs[:, :qkv_tile].reshape(w_qkv.shape),
        pairs[:, qkv_tile:],
        out_up,
        out_down,
        grad_ada,
        grad_table,
    )


def solution(mesh):
    rows = P(None, "dp", None, "tensor", None)
    weight = P("dp", "tensor")
    qkv_weight = P("dp", None, "tensor")
    cond = P(None, "dp", None)
    table = P("tensor", None)
    return jax.shard_map(
        functools.partial(body, mesh.shape["dp"], mesh.shape["tensor"]),
        mesh=mesh,
        in_specs=(rows, cond, P(None, "dp"), qkv_weight, weight, weight, weight, weight, table, rows),
        out_specs=(rows, rows, cond, qkv_weight, weight, weight, weight, weight, table),
        check_vma=False,
    )
```
